768 devices in a mesh: group: 16 (over y_hi, x), tile: 48 (over z, y_lo, core).
Axes of the slice: x: 4, y: 8 (y_hi: 4, y_lo: 2; y = y_hi * 2 + y_lo), z: 12, core: 2. Of those that a mesh axis runs over, the one named last changes fastest.
Arguments:
- tracer: float32 [16, 256, 12288], P(None, 'group', 'tile'), may hold values from -6 to 6
- east_speed: float32 [16, 256, 12288], P(None, 'group', 'tile'), may hold values from -0.5 to 0.5
- north_speed: float32 [16, 256, 12288], P(None, 'group', 'tile'), may hold values from -0.5 to 0.5
- mixing: float32 [15, 256, 12288], P(None, 'group', 'tile'), may hold values from 0.1 to 3
- depth_levels: int32 [256, 12288], P('group', 'tile'), may hold values from 0 to 16
- sensitivity: float32 [16, 256, 12288], P(None, 'group', 'tile'), may hold values from -6 to 6
Outputs:
- final_state: float32 [16, 256, 12288], P(None, 'group', 'tile')
- adjoint_state: float32 [16, 256, 12288], P(None, 'group', 'tile')
The draws below stay inside these ranges and needn't reach their ends.
All inputs are finite; a program needn't handle non-finite values.
Results may differ from the reference program's by a relative error of at most 0.0001.
Values sent between devices are 32-bit elements; how exact they have to be, the bound alone decides.
A program may use at most 32 MiB of HBM per device.

```python
import math
import jax
import jax.numpy as jnp
from jax import lax

NZ = 16
NZM = 15
NY = 256
NX = 12288


def signed_speed(key, salt):
    mixed_key = jax.random.fold_in(key, salt)
    sign_key, size_key = jax.random.split(mixed_key)
    shape = (NZ, NY, NX)
    signs = (jax.random.randint(sign_key, shape, 0, 2) * 2 - 1).astype(jnp.float32)
    magnitude = jax.random.uniform(size_key, shape, jnp.float32, 0.35, 0.5)
    return (signs * magnitude).astype(jnp.float32)


def draw_east_speed(key, part):
    return signed_speed(key, 7101)


def draw_north_speed(key, part):
    return signed_speed(key, 7202)


def draw_depth_levels(key, part):
    mixed_key = jax.random.fold_in(key, 7303)
    choose_key, level_key = jax.random.split(mixed_key)
    shape = (NY, NX)
    choose_full = jax.random.randint(choose_key, shape, 0, 4)
    shallow = jax.random.randint(level_key, shape, 0, NZ + 1)
    depth = jnp.where(choose_full != 0, NZ, shallow).astype(jnp.int32)
    row_index = lax.broadcasted_iota(jnp.int32, shape, 0)
    column_index = lax.broadcasted_iota(jnp.int32, shape, 1)
    planted = jnp.logical_and(row_index == 0, column_index == 0)
    return jnp.where(planted, 0, depth).astype(jnp.int32)


def block_scale(key, dims, pieces, least, largest):
    factor_of = 1.0
    for axis_at, parts in pieces:
        heights = jax.random.uniform(jax.random.fold_in(jax.random.fold_in(key, 6), axis_at), (parts,), jnp.float32, least / len(pieces), largest / len(pieces))
        factor_of = factor_of * jnp.repeat(jnp.exp(heights), dims[axis_at] // parts).reshape((-1,) + (1,) * (len(dims) - 1 - axis_at))
    return factor_of


def centred(key, shape, deviation, limit, shards=(), kind=jnp.bfloat16):
    entries = deviation * jax.random.normal(key, shape, jnp.float32)
    if shards:
        entries = entries * block_scale(key, shape, shards, -0.22, 0.18)
    return jnp.clip(entries, -limit, limit).astype(kind)


def setup_inputs(seed: int = 0) -> dict:
    splits = jax.random.split(jax.random.key(seed), 7)
    tracer = centred(splits[0], (NZ, NY, NX), 1.0, 6.0, ((1, 16), (2, 48)), jnp.float32)
    east_speed = draw_east_speed(jax.random.fold_in(splits[6], 71), 0)
    north_speed = draw_north_speed(jax.random.fold_in(splits[6], 71), 0)
    mixing = jnp.clip(jnp.exp(math.log(3.0) - 3.4011974 * jax.random.uniform(splits[3], (NZM, NY, NX), jnp.float32) ** block_scale(splits[3], (NZM, NY, NX), ((1, 16), (2, 48)), -0.2, 0.2)), 0.1, 3.0)
    depth_levels = draw_depth_levels(jax.random.fold_in(splits[6], 71), 0)
    sensitivity = centred(splits[5], (NZ, NY, NX), 1.0, 6.0, ((1, 16), (2, 48)), jnp.float32)
    return dict(tracer=tracer, east_speed=east_speed, north_speed=north_speed, mixing=mixing, depth_levels=depth_levels, sensitivity=sensitivity)


diffusivity = 0.1
uptake = 0.2


def interval(source, first_index, last_index, along_axis):
    return lax.slice_in_dim(source, first_index, last_index, axis=along_axis)


def trim_margin(source, margin):
    if margin == 0:
        return source
    return source[:, margin:source.shape[1] - margin, margin:source.shape[2] - margin]


def flux_change(tracer_field, face_speed, wet_mask, along_axis):
    extent = tracer_field.shape[along_axis]
    open_face = interval(wet_mask, 2, extent - 1, along_axis) * interval(wet_mask, 1, extent - 2, along_axis)
    inner = interval(tracer_field, 2, extent - 1, along_axis)
    behind = interval(tracer_field, 1, extent - 2, along_axis)
    outer = interval(tracer_field, 3, extent, along_axis) + interval(tracer_field, 0, extent - 3, along_axis)
    face_flux = open_face * (interval(face_speed, 2, extent - 1, along_axis) * (7.0 * (inner + behind) - outer) / 12.0 - diffusivity * (inner - behind))
    faces_total = face_flux.shape[along_axis]
    return interval(face_flux, 0, faces_total - 1, along_axis) - interval(face_flux, 1, faces_total, along_axis)


def explicit_step(tracer_field, east_face, north_face, wet_mask):
    across = flux_change(tracer_field, east_face, wet_mask, 2)
    across = across[:, 2:across.shape[1] - 2, :]
    north_term = flux_change(tracer_field, north_face, wet_mask, 1)
    north_term = north_term[:, :, 2:north_term.shape[2] - 2]
    middle = trim_margin(tracer_field, 2)
    return trim_margin(wet_mask, 2) * (middle + across + north_term - uptake * middle * middle)


def flux_reverse(weight, face_speed, wet_mask, along_axis):
    extent = weight.shape[along_axis]
    open_face = interval(wet_mask, 1, extent, along_axis) * interval(wet_mask, 0, extent - 1, along_axis)
    face_jump = interval(weight, 1, extent, along_axis) - interval(weight, 0, extent - 1, along_axis)
    carried = open_face * interval(face_speed, 1, extent, along_axis) * face_jump / 12.0
    spread = diffusivity * open_face * face_jump
    face_count = extent - 1
    moved = 7.0 * (interval(carried, 1, face_count - 2, along_axis) + interval(carried, 2, face_count - 1, along_axis)) - interval(carried, 0, face_count - 3, along_axis) - interval(carried, 3, face_count, along_axis)
    mixed = interval(spread, 2, face_count - 1, along_axis) - interval(spread, 1, face_count - 2, along_axis)
    return moved + mixed


def adjoint_explicit(weight, state_now, east_face, north_face, wet_mask):
    across = flux_reverse(weight, east_face, wet_mask, 2)
    across = across[:, 2:across.shape[1] - 2, :]
    north_term = flux_reverse(weight, north_face, wet_mask, 1)
    north_term = north_term[:, :, 2:north_term.shape[2] - 2]
    middle = trim_margin(weight, 2)
    return middle + across + north_term - 2.0 * uptake * state_now * middle


def factorize(mixing_field, wet_mask):
    links = mixing_field * wet_mask[:-1] * wet_mask[1:]
    layers = wet_mask.shape[0]
    zero_plane = jnp.zeros_like(wet_mask[0])
    uppers = []
    inverses = []
    above_link = zero_plane
    above_upper = zero_plane
    for position in range(layers):
        below_link = links[position] if position < layers - 1 else zero_plane
        pivot_sum = 1.0 + above_link + below_link + above_link * above_upper
        inverse = 1.0 / pivot_sum
        upper_term = -below_link * inverse
        uppers.append(upper_term)
        inverses.append(inverse)
        above_link = below_link
        above_upper = upper_term
    return jnp.stack(uppers), jnp.stack(inverses), links


def column_solve(factors, right_side):
    uppers, inverses, links = factors
    layers = right_side.shape[0]
    current = right_side[0] * inverses[0]
    forward_pass = [current]
    for position in range(1, layers):
        current = (right_side[position] + links[position - 1] * current) * inverses[position]
        forward_pass.append(current)
    result = [current]
    for position in range(layers - 2, -1, -1):
        current = forward_pass[position] - uppers[position] * current
        result.append(current)
    return jnp.stack(result[::-1])


def pad_zero(source, margin):
    return jnp.pad(source, ((0, 0), (margin, margin), (margin, margin)))


def reference(tracer, east_speed, north_speed, mixing, depth_levels, sensitivity):
    levels = jnp.arange(tracer.shape[0], dtype=jnp.int32)[:, None, None]
    wet_mask = jnp.where(levels < depth_levels[None], 1.0, 0.0).astype(tracer.dtype)
    factors = factorize(mixing, wet_mask)
    east_pad = pad_zero(east_speed, 2)
    north_pad = pad_zero(north_speed, 2)
    wet_pad = pad_zero(wet_mask, 2)
    first_state = column_solve(factors, explicit_step(pad_zero(tracer, 2), east_pad, north_pad, wet_pad))
    final_state = column_solve(factors, explicit_step(pad_zero(first_state, 2), east_pad, north_pad, wet_pad))
    adjoint = sensitivity
    for state_now in (first_state, tracer):
        gradient = wet_mask * column_solve(factors, adjoint)
        adjoint = adjoint_explicit(pad_zero(gradient, 2), state_now, east_pad, north_pad, wet_pad)
    return final_state, adjoint
```

```python
import functools

import jax
import jax.numpy as jnp
from jax import lax
from jax.experimental import pallas as pl
from jax.experimental.pallas import tpu as pltpu
from jax.sharding import PartitionSpec as P

F32 = jnp.float32
MESH_ID = pl.DeviceIdType.MESH
LEV = 16
ROWS = 16
FLAT = LEV * ROWS
PAD = 8
PR = FLAT + 2 * PAD
TWELFTH = 1.0 / 12.0
UNROLL = 2


def roll(x, shift, axis):
    n = x.shape[axis]
    return pltpu.roll(x, shift % n, axis)


def kernel(
    n_group, n_tile,
    tr_hbm, es_hbm, ns_hbm, mx_hbm, dep_hbm, se_hbm,
    fin_hbm, adj_hbm,
    cbuf, ebuf, xbuf, ybuf, mbuf, gbuf, rbuf, fbuf, hbuf, ibuf, dbuf, sbuf, g2buf, qbuf,
    dn_e, up_e, dn_l, up_l, dn_a, up_a, dn_b, up_b, px_e, px_l, px_a, px_b,
    ru_e, rd_e, ru_l, rd_l, ru_a, rd_a, ru_b, rd_b,
    rl_e, rr_e, rl_l, rr_l, rl_a, rr_a, rl_b, rr_b,
    in_sem, out_sem, send_sem, recv_sem,
):
    gi = lax.axis_index("group")
    ti = lax.axis_index("tile")
    up_id = lax.rem(gi + n_group - 1, n_group)
    dn_id = lax.rem(gi + 1, n_group)
    lf_id = lax.rem(ti + n_tile - 1, n_tile)
    rt_id = lax.rem(ti + 1, n_tile)
    targets = {"up": (up_id, ti), "dn": (dn_id, ti), "lf": (gi, lf_id), "rt": (gi, rt_id)}

    barrier = pltpu.get_barrier_semaphore()
    for who in ("up", "dn", "lf", "rt"):
        pl.semaphore_signal(barrier, inc=1, device_id=targets[who], device_id_type=MESH_ID)

    keep_u = jnp.where(gi == 0, 0.0, 1.0).astype(F32)
    keep_d = jnp.where(gi == n_group - 1, 0.0, 1.0).astype(F32)
    keep_l = jnp.where(ti == 0, 0.0, 1.0).astype(F32)
    keep_r = jnp.where(ti == n_tile - 1, 0.0, 1.0).astype(F32)

    def fetch(src, dst, base, rows, sem):
        out = []
        for t in range(2):
            out.append(pltpu.make_async_copy(
                src.at[:, pl.ds(128 * t, 128)], dst.at[pl.ds(t * base[1] + base[0], rows), :], in_sem.at[sem, t]))
        for copy in out:
            copy.start()
        return out

    pad = (PAD, PR)
    cp_dep = fetch(dep_hbm, dbuf, (0, ROWS), ROWS, 0)
    cp_mx = fetch(mx_hbm, mbuf, pad, FLAT - ROWS, 1)
    cp_se = fetch(se_hbm, sbuf, pad, FLAT, 2)
    cp_tr = fetch(tr_hbm, cbuf, pad, FLAT, 3)
    cp_ns = fetch(ns_hbm, ybuf, pad, FLAT, 4)
    cp_es = fetch(es_hbm, xbuf, pad, FLAT, 5)

    def wait_all(copies):
        for copy in copies:
            copy.wait()

    row16 = lax.broadcasted_iota(jnp.int32, (16, 128), 0)
    lane16 = lax.broadcasted_iota(jnp.int32, (16, 128), 1)
    lane8 = lax.broadcasted_iota(jnp.int32, (8, 128), 1)
    levrow = row16.astype(F32)
    slot = lane8 // 4
    part = lane8 % 4
    levlane = (lane8 // 8).astype(F32)

    def get(ref, t, lev, shift=0):
        return ref[pl.ds(t * PR + PAD + 16 * lev + shift, 16), :]

    def put(ref, t, lev, value):
        ref[pl.ds(t * PR + PAD + 16 * lev, 16), :] = value

    def row_of(ref, t, r):
        return ref[pl.ds(t * PR + PAD + r, LEV, stride=ROWS), :]

    def row_add(ref, t, r, value):
        where = pl.ds(t * PR + PAD + r, LEV, stride=ROWS)
        ref[where, :] = ref[where, :] + value

    zero_pad = jnp.zeros((8, 128), F32)
    for ref in (cbuf, gbuf, ebuf, g2buf):
        for t in range(2):
            ref[pl.ds(t * PR, PAD), :] = zero_pad
            ref[pl.ds(t * PR + PAD + FLAT, PAD), :] = zero_pad

    def pack_tiles(read):
        acc = jnp.zeros((8, 128), F32)
        for k in range(32):
            left, right = read(k)
            merged = jnp.where(lane8 < 64, left, right)
            acc = jnp.where(slot == k, roll(merged, 4 * k + 2, 1), acc)
        return acc

    def pack(ref):
        return pack_tiles(lambda k: (
            ref[pl.ds(PAD + 8 * k, 8), :], ref[pl.ds(PR + PAD + 8 * k, 8), :]))

    wait_all(cp_dep)
    dep = [dbuf[pl.ds(16 * t, 16), :].astype(F32) for t in range(2)]
    dm_y = [jnp.where(row16 == 0, 0.0, jnp.minimum(dep[t], roll(dep[t], 1, 0))) for t in range(2)]
    dr = [roll(dep[t], 1, 1) for t in range(2)]
    dm_x = [jnp.where(lane16 == 0, 0.0, jnp.minimum(dep[0], dr[0])),
            jnp.minimum(dep[1], jnp.where(lane16 == 0, dr[0], dr[1]))]
    dp = jnp.zeros((8, 128), F32)
    for k in range(2):
        merged = jnp.where(lane8 < 64, dep[0][8 * k:8 * k + 8], dep[1][8 * k:8 * k + 8])
        dp = jnp.where(slot == k, roll(merged, 4 * k + 2, 1), dp)
    for width in (8, 16, 32, 64):
        dp = dp + roll(dp, width, 1)
    for t in range(2):
        dn_e[pl.ds(64 + 8 * t, 8), :] = jnp.broadcast_to(dep[t][15:16, :], (8, 128))
        up_e[pl.ds(96 + 8 * t, 8), :] = jnp.broadcast_to(dep[t][0:1, :], (8, 128))

    wait_all(cp_mx)
    above = [None, None]
    fprev = [None, None]
    for lev in range(LEV):
        for t in range(2):
            if lev < LEV - 1:
                below = jnp.where(dep[t] > lev + 1.0, get(mbuf, t, lev), 0.0)
            else:
                below = jnp.zeros((16, 128), F32)
            if lev == 0:
                pivot = 1.0 + below
            else:
                pivot = (1.0 + below) + above[t] * (1.0 - fprev[t])
            inv = 1.0 / pivot
            put(ibuf, t, lev, inv)
            if lev > 0:
                put(hbuf, t, lev, above[t] * inv)
            above[t] = below
            fprev[t] = below * inv
            put(fbuf, t, lev, fprev[t])

    def backward(ref, last, finish, out_ref):
        cur = last
        for t in range(2):
            put(out_ref, t, LEV - 1, finish(t, LEV - 1, cur[t]))
        for lev in range(LEV - 2, -1, -1):
            for t in range(2):
                cur[t] = get(ref, t, lev) + get(fbuf, t, lev) * cur[t]
                put(out_ref, t, lev, finish(t, lev, cur[t]))

    def forward(read, ref):
        cur = [None, None]
        for lev in range(LEV):
            rhs = read(lev)
            for t in range(2):
                value = rhs[t] * get(ibuf, t, lev)
                if lev > 0:
                    value = value + get(hbuf, t, lev) * cur[t]
                cur[t] = value
                put(ref, t, lev, value)
        return cur

    def masked(t, lev, value):
        return jnp.where(dep[t] > lev, value, 0.0)

    wait_all(cp_se)
    last = forward(lambda lev: [get(sbuf, t, lev) for t in range(2)], qbuf)
    backward(qbuf, last, masked, gbuf)

    wait_all(cp_tr)
    wait_all(cp_ns)
    wait_all(cp_es)
    c_rows = {r: [row_of(cbuf, t, r) for t in range(2)] for r in (0, 1, 14, 15)}
    s_rows = {r: [row_of(ybuf, t, r) for t in range(2)] for r in (0, 1, 15)}
    d_rows = {r: [jnp.broadcast_to(dep[t][r:r + 1, :], (16, 128)) for t in range(2)] for r in (0, 1, 14, 15)}
    for t in range(2):
        dn_e[pl.ds(16 * t, 16), :] = c_rows[14][t]
        dn_e[pl.ds(32 + 16 * t, 16), :] = c_rows[15][t]
        up_e[pl.ds(16 * t, 16), :] = c_rows[0][t]
        up_e[pl.ds(32 + 16 * t, 16), :] = c_rows[1][t]
        up_e[pl.ds(64 + 16 * t, 16), :] = s_rows[0][t]
    c_pk = pack(cbuf)
    s_pk = pack(xbuf)
    px_e[pl.ds(0, 8), :] = c_pk
    px_e[pl.ds(8, 8), :] = s_pk
    px_e[pl.ds(16, 8), :] = dp

    a1 = [jnp.where(jnp.minimum(d_rows[0][t], d_rows[1][t]) > levrow, s_rows[1][t], 0.0) for t in range(2)]
    a15 = [jnp.where(jnp.minimum(d_rows[14][t], d_rows[15][t]) > levrow, s_rows[15][t], 0.0) for t in range(2)]
    a_pk = jnp.where(jnp.minimum(dp, roll(dp, 1, 1)) > levlane, s_pk, 0.0)

    def edge_rows(ref):
        return {r: [row_of(ref, t, r) for t in range(2)] for r in (0, 1, 14, 15)}

    def stage_gradient(ref, dn, up, px):
        rows = edge_rows(ref)
        for t in range(2):
            dn[pl.ds(16 * t, 16), :] = rows[15][t]
            dn[pl.ds(32 + 16 * t, 16), :] = a15[t] * (rows[15][t] - rows[14][t])
            up[pl.ds(16 * t, 16), :] = rows[0][t]
            up[pl.ds(32 + 16 * t, 16), :] = a1[t] * (rows[1][t] - rows[0][t])
        packed = pack(ref)
        px[pl.ds(0, 8), :] = packed
        px[pl.ds(8, 8), :] = a_pk * (packed - roll(packed, 1, 1))
        return rows, packed

    g_rows, g_pk = stage_gradient(gbuf, dn_l, up_l, px_l)

    def message(index, srcs, dsts):
        copies = {}
        for d, who in enumerate(("up", "dn", "lf", "rt")):
            copies[who] = pltpu.make_async_remote_copy(
                src_ref=srcs[who], dst_ref=dsts[who],
                send_sem=send_sem.at[index, d], recv_sem=recv_sem.at[index, d],
                device_id=targets[who], device_id_type=MESH_ID)
        for who in ("up", "dn", "lf", "rt"):
            copies[who].start()
        return copies

    pl.semaphore_wait(barrier, 4)
    msg_e = message(0, {"up": up_e, "dn": dn_e, "lf": px_e, "rt": px_e},
                    {"up": rd_e, "dn": ru_e, "lf": rr_e, "rt": rl_e})
    msg_l = message(1, {"up": up_l, "dn": dn_l, "lf": px_l, "rt": px_l},
                    {"up": rd_l, "dn": ru_l, "lf": rr_l, "rt": rl_l})

    def arrive(copies):
        for who in ("lf", "rt", "up", "dn"):
            copies[who].wait_recv()

    lane0 = lane16 == 0
    lane127 = lane16 == 127
    lane_lo2 = lane16 < 2
    lane_hi2 = lane16 >= 126
    row0 = row16 == 0
    row15 = row16 == 15
    row_lo2 = row16 < 2
    row_hi2 = row16 >= 14

    def explicit_level(src, lev, dst):
        level = lax.convert_element_type(lev, F32) if not isinstance(lev, int) else float(lev)
        c = [get(src, t, lev) for t in range(2)]
        r1 = [roll(c[t], 1, 1) for t in range(2)]
        r2 = [roll(c[t], 2, 1) for t in range(2)]
        q1 = [roll(c[t], 127, 1) for t in range(2)]
        m1 = [r1[0], jnp.where(lane0, r1[0], r1[1])]
        m2 = [jnp.where(lane_lo2, 0.0, r2[0]), jnp.where(lane_lo2, r2[0], r2[1])]
        p1 = [jnp.where(lane127, q1[1], q1[0]), jnp.where(lane127, 0.0, q1[1])]
        gx = [jnp.where(dm_x[t] > level,
                        get(xbuf, t, lev) * (7.0 * (c[t] + m1[t]) - (p1[t] + m2[t])) - 1.2 * (c[t] - m1[t]), 0.0)
              for t in range(2)]
        h1 = [roll(gx[t], 127, 1) for t in range(2)]
        gxp = [jnp.where(lane127, h1[1], h1[0]), jnp.where(lane127, h1[0], h1[1])]
        for t in range(2):
            ym1 = get(src, t, lev, -1)
            ym2 = jnp.where(row_lo2, 0.0, get(src, t, lev, -2))
            yp1 = jnp.where(row15, 0.0, get(src, t, lev, 1))
            gy = jnp.where(dm_y[t] > level,
                           get(ybuf, t, lev) * (7.0 * (c[t] + ym1) - (yp1 + ym2)) - 1.2 * (c[t] - ym1), 0.0)
            gyp = roll(gy, 15, 0)
            put(dst, t, lev, c[t] * (1.0 - 0.2 * c[t]) + ((gx[t] - gxp[t]) + (gy - gyp)) * TWELFTH)

    def adjoint_level(src, lev, dst, extra):
        level = lax.convert_element_type(lev, F32) if not isinstance(lev, int) else float(lev)
        g = [get(src, t, lev) for t in range(2)]
        r1 = [roll(g[t], 1, 1) for t in range(2)]
        m1 = [r1[0], jnp.where(lane0, r1[0], r1[1])]
        j = [jnp.where(dm_x[t] > level, g[t] - m1[t], 0.0) for t in range(2)]
        cx = [get(xbuf, t, lev) * j[t] for t in range(2)]
        u = [7.0 * cx[t] + 1.2 * j[t] for t in range(2)]
        w = [7.0 * cx[t] - 1.2 * j[t] for t in range(2)]
        u1 = [roll(u[t], 127, 1) for t in range(2)]
        up1 = [jnp.where(lane127, u1[1], u1[0]), jnp.where(lane127, 0.0, u1[1])]
        k1 = [roll(cx[t], 1, 1) for t in range(2)]
        cm1 = [jnp.where(lane0, 0.0, k1[0]), jnp.where(lane0, k1[0], k1[1])]
        k2 = [roll(cx[t], 126, 1) for t in range(2)]
        cp2 = [jnp.where(lane_hi2, k2[1], k2[0]), jnp.where(lane_hi2, 0.0, k2[1])]
        for t in range(2):
            jy = jnp.where(dm_y[t] > level, g[t] - get(src, t, lev, -1), 0.0)
            cy = get(ybuf, t, lev) * jy
            uy = 7.0 * cy + 1.2 * jy
            wy = 7.0 * cy - 1.2 * jy
            uyp = roll(uy, 15, 0)
            cym = jnp.where(row0, 0.0, roll(cy, 1, 0))
            cyp = jnp.where(row_hi2, 0.0, roll(cy, 14, 0))
            total = ((w[t] + up1[t]) - (cm1[t] + cp2[t])) + ((wy + uyp) - (cym + cyp))
            put(dst, t, lev, extra(t, lev, g[t]) + total * TWELFTH)

    def over_levels(body):
        def step(i, carry):
            for u in range(UNROLL):
                body(i * UNROLL + u)
            return carry
        lax.fori_loop(0, LEV // UNROLL, step, 0)

    over_levels(lambda lev: explicit_level(cbuf, lev, ebuf))
    over_levels(lambda lev: adjoint_level(gbuf, lev, rbuf, lambda t, l, g: g))

    arrive(msg_e)
    du = [jnp.concatenate([ru_e[pl.ds(64 + 8 * t, 8), :]] * 2, axis=0) * keep_u for t in range(2)]
    dd = [jnp.concatenate([rd_e[pl.ds(96 + 8 * t, 8), :]] * 2, axis=0) * keep_d for t in range(2)]
    open0 = [jnp.minimum(du[t], d_rows[0][t]) > levrow for t in range(2)]
    openn = [jnp.minimum(dd[t], d_rows[15][t]) > levrow for t in range(2)]
    a0 = [jnp.where(open0[t], s_rows[0][t], 0.0) for t in range(2)]
    an = [jnp.where(openn[t], rd_e[pl.ds(64 + 16 * t, 16), :], 0.0) for t in range(2)]
    b0 = [jnp.where(open0[t], 1.2, 0.0) for t in range(2)]
    bn = [jnp.where(openn[t], 1.2, 0.0) for t in range(2)]
    is2 = part == 2
    low = part < 2
    sp_l = rl_e[pl.ds(8, 8), :]
    sp_r = rr_e[pl.ds(8, 8), :]
    dp_l = rl_e[pl.ds(16, 8), :] * keep_l
    dp_r = rr_e[pl.ds(16, 8), :] * keep_r
    d_near = jnp.where(low, roll(dp_r, -1, 1), roll(dp_l, 1, 1))
    open_pk = jnp.minimum(dp, d_near) > levlane
    af_pk = jnp.where(open_pk, jnp.where(low, roll(sp_r, -1, 1), s_pk), 0.0)
    bf_pk = jnp.where(open_pk, 1.2, 0.0)
    a_next = roll(a_pk, -1, 1)

    def explicit_rows(ref, rows, ru, rd):
        for t in range(2):
            c2 = ru[pl.ds(16 * t, 16), :] * keep_u
            c1 = ru[pl.ds(32 + 16 * t, 16), :] * keep_u
            n0 = rd[pl.ds(16 * t, 16), :] * keep_d
            n1 = rd[pl.ds(32 + 16 * t, 16), :] * keep_d
            r0, r1, r14, r15 = (rows[r][t] for r in (0, 1, 14, 15))
            g0 = a0[t] * (7.0 * (r0 + c1) - (r1 + c2)) - b0[t] * (r0 - c1)
            gn = an[t] * (7.0 * (n0 + r15) - (n1 + r14)) - bn[t] * (n0 - r15)
            p = a1[t] * c1
            q = a15[t] * n0
            row_add(ref, t, 0, (g0 + p) * TWELFTH)
            row_add(ref, t, 1, p * -TWELFTH)
            row_add(ref, t, 14, q * TWELFTH)
            row_add(ref, t, 15, (q + gn) * -TWELFTH)

    def explicit_cols(c, rl, rr):
        cl = rl[pl.ds(0, 8), :] * keep_l
        cr = rr[pl.ds(0, 8), :] * keep_r
        x1, x2 = roll(cl, 1, 1), roll(cl, 2, 1)
        y1, y2 = roll(cr, -1, 1), roll(cr, -2, 1)
        near = jnp.where(low, y1, x1)
        far = jnp.where(low, y2 + roll(c, 1, 1), x2 + roll(c, -1, 1))
        step = jnp.where(low, y1 - c, c - x1)
        face = af_pk * (7.0 * (c + near) - far) - bf_pk * step
        return TWELFTH * jnp.where(
            part == 0, a_next * y2,
            jnp.where(part == 1, -(a_pk * y1 + face),
                      jnp.where(part == 2, face + a_next * x1, -(a_pk * x2))))

    def adjoint_rows(ref, rows, ru, rd):
        for t in range(2):
            gu = ru[pl.ds(16 * t, 16), :] * keep_u
            cu = ru[pl.ds(32 + 16 * t, 16), :] * keep_u
            gd = rd[pl.ds(16 * t, 16), :] * keep_d
            cd = rd[pl.ds(32 + 16 * t, 16), :] * keep_d
            j0 = rows[0][t] - gu
            jn = gd - rows[15][t]
            f0 = a0[t] * j0
            fn = an[t] * jn
            row_add(ref, t, 0, (7.0 * f0 - cu - b0[t] * j0) * TWELFTH)
            row_add(ref, t, 1, f0 * -TWELFTH)
            row_add(ref, t, 14, fn * -TWELFTH)
            row_add(ref, t, 15, (7.0 * fn - cd + bn[t] * jn) * TWELFTH)

    def adjoint_cols(g, rl, rr):
        gl = rl[pl.ds(0, 8), :] * keep_l
        kl = rl[pl.ds(8, 8), :] * keep_l
        gr = rr[pl.ds(0, 8), :] * keep_r
        kr = rr[pl.ds(8, 8), :] * keep_r
        j = jnp.where(low, roll(gr, -1, 1) - g, g - roll(gl, 1, 1))
        f = af_pk * j
        s = bf_pk * j
        outer = jnp.where(low, roll(kr, -2, 1), roll(kl, 1, 1))
        edge = 7.0 * f - outer + jnp.where(low, s, -s)
        inner = -jnp.where(low, roll(f, -1, 1), roll(f, 1, 1))
        return TWELFTH * jnp.where((part == 1) | is2, edge, inner)

    lane_lo2_8 = lane8 < 2
    lane_hi2_8 = lane8 >= 126

    def with_cols(ref, packed, lev):
        halves = [roll(packed, 126 - 4 * (2 * lev + k), 1) for k in range(2)]
        left = jnp.concatenate([jnp.where(lane_lo2_8, h, 0.0) for h in halves], axis=0)
        right = jnp.concatenate([jnp.where(lane_hi2_8, h, 0.0) for h in halves], axis=0)
        return [get(ref, 0, lev) + left, get(ref, 1, lev) + right]

    def solve_explicit(packed, out_ref):
        def read(lev):
            both = with_cols(ebuf, packed, lev)
            return [masked(t, lev, both[t]) for t in range(2)]
        last = forward(read, qbuf)
        backward(qbuf, last, lambda t, lev, v: v, out_ref)

    explicit_rows(ebuf, c_rows, ru_e, rd_e)
    solve_explicit(explicit_cols(c_pk, rl_e, rr_e), sbuf)

    f_rows = edge_rows(sbuf)
    f_pk = pack(sbuf)
    for t in range(2):
        dn_a[pl.ds(16 * t, 16), :] = f_rows[14][t]
        dn_a[pl.ds(32 + 16 * t, 16), :] = f_rows[15][t]
        up_a[pl.ds(16 * t, 16), :] = f_rows[0][t]
        up_a[pl.ds(32 + 16 * t, 16), :] = f_rows[1][t]
    px_a[...] = f_pk
    msg_a = message(2, {"up": up_a, "dn": dn_a, "lf": px_a, "rt": px_a},
                    {"up": rd_a, "dn": ru_a, "lf": rr_a, "rt": rl_a})

    arrive(msg_l)
    adjoint_rows(rbuf, g_rows, ru_l, rd_l)
    packed = adjoint_cols(g_pk, rl_l, rr_l)

    def read_adjoint(lev):
        both = with_cols(rbuf, packed, lev)
        return [both[t] - 0.4 * get(sbuf, t, lev) * get(gbuf, t, lev) for t in range(2)]

    last = forward(read_adjoint, qbuf)
    backward(qbuf, last, masked, g2buf)
    h_rows, h_pk = stage_gradient(g2buf, dn_b, up_b, px_b)
    msg_b = message(3, {"up": up_b, "dn": dn_b, "lf": px_b, "rt": px_b},
                    {"up": rd_b, "dn": ru_b, "lf": rr_b, "rt": rl_b})

    over_levels(lambda lev: explicit_level(sbuf, lev, ebuf))
    over_levels(lambda lev: adjoint_level(
        g2buf, lev, rbuf, lambda t, l, g: g * (1.0 - 0.4 * get(cbuf, t, l))))

    arrive(msg_a)
    explicit_rows(ebuf, f_rows, ru_a, rd_a)
    solve_explicit(explicit_cols(f_pk, rl_a, rr_a), gbuf)

    def flush(src, dst, sem):
        out = []
        for t in range(2):
            out.append(pltpu.make_async_copy(
                src.at[pl.ds(t * PR + PAD, FLAT), :], dst.at[:, pl.ds(128 * t, 128)], out_sem.at[sem, t]))
        for copy in out:
            copy.start()
        return out

    cp_fin = flush(gbuf, fin_hbm, 0)

    arrive(msg_b)
    adjoint_rows(rbuf, h_rows, ru_b, rd_b)
    packed_b = adjoint_cols(h_pk, rl_b, rr_b)
    for lev in range(LEV):
        both = with_cols(rbuf, packed_b, lev)
        for t in range(2):
            put(rbuf, t, lev, both[t])
    cp_adj = flush(rbuf, adj_hbm, 1)

    for msg in (msg_e, msg_l, msg_a, msg_b):
        for who in ("up", "dn", "lf", "rt"):
            msg[who].wait_send()
    wait_all(cp_fin)
    wait_all(cp_adj)


def solution(mesh):
    n_group, n_tile = mesh.shape["group"], mesh.shape["tile"]

    def shards(tracer, east_speed, north_speed, mixing, depth_levels, sensitivity):
        lev, rows, cols = tracer.shape

        def flat(x):
            return x.reshape(-1, cols)

        def vm(n):
            return pltpu.VMEM((n, 128), F32)

        big = 2 * PR
        hbm = pl.BlockSpec(memory_space=pl.ANY)
        out = pl.pallas_call(
            functools.partial(kernel, n_group, n_tile),
            out_shape=[jax.ShapeDtypeStruct((lev * rows, cols), F32)] * 2,
            in_specs=[hbm] * 6,
            out_specs=[hbm] * 2,
            scratch_shapes=(
                [vm(big)] * 10 + [pltpu.VMEM((32, 128), jnp.int32)] + [vm(big)] * 3
                + [vm(80), vm(112), vm(64), vm(64), vm(64), vm(64), vm(64), vm(64)]
                + [vm(24), vm(16), vm(8), vm(16)]
                + [vm(80), vm(112), vm(64), vm(64), vm(64), vm(64), vm(64), vm(64)]
                + [vm(24), vm(24), vm(16), vm(16), vm(8), vm(8), vm(16), vm(16)]
                + [pltpu.SemaphoreType.DMA((6, 2)), pltpu.SemaphoreType.DMA((2, 2)),
                   pltpu.SemaphoreType.DMA((4, 4)), pltpu.SemaphoreType.DMA((4, 4))]
            ),
            compiler_params=pltpu.CompilerParams(collective_id=0, has_side_effects=True),
        )(flat(tracer), flat(east_speed), flat(north_speed), flat(mixing), depth_levels, flat(sensitivity))
        return tuple(o.reshape(lev, rows, cols) for o in out)

    spec = P(None, "group", "tile")
    return jax.shard_map(
        shards, mesh=mesh, in_specs=(spec, spec, spec, spec, P("group", "tile"), spec),
        out_specs=(spec, spec), check_vma=False)
```

```python
import functools

import jax
import jax.numpy as jnp
from jax import lax
from jax.experimental import pallas as pl
from jax.experimental.pallas import tpu as pltpu
from jax.sharding import PartitionSpec as P

F32 = jnp.float32
MESH_ID = pl.DeviceIdType.MESH
LEV = 16
ROWS = 16
FLAT = LEV * ROWS
PAD = 8
PR = FLAT + 2 * PAD
TWELFTH = 1.0 / 12.0
UNROLL = 16
VMEM_MAIN = 32 * 2**20
VMEM_FLUSH = 8 * 2**20


def roll(x, shift, axis):
    n = x.shape[axis]
    return pltpu.roll(x, shift % n, axis)


def kernel(
    n_group, n_tile,
    tr_hbm, es_hbm, ns_hbm, mx_hbm, dep_hbm, se_hbm,
    final, rbuf,
    cbuf, ebuf, xbuf, ybuf, mbuf, gbuf, fbuf, hbuf, ibuf, dbuf, sbuf, g2buf, qbuf,
    dn_e, up_e, dn_l, up_l, dn_a, up_a, dn_b, up_b, px_e, px_l, px_a, px_b,
    ru_e, rd_e, ru_l, rd_l, ru_a, rd_a, ru_b, rd_b,
    rl_e, rr_e, rl_l, rr_l, rl_a, rr_a, rl_b, rr_b,
    in_sem, send_sem, recv_sem,
):
    gi = lax.axis_index("group")
    ti = lax.axis_index("tile")
    up_id = lax.rem(gi + n_group - 1, n_group)
    dn_id = lax.rem(gi + 1, n_group)
    lf_id = lax.rem(ti + n_tile - 1, n_tile)
    rt_id = lax.rem(ti + 1, n_tile)
    targets = {"up": (up_id, ti), "dn": (dn_id, ti), "lf": (gi, lf_id), "rt": (gi, rt_id)}

    has = {"up": gi > 0, "dn": gi < n_group - 1, "lf": ti > 0, "rt": ti < n_tile - 1}
    opposite = {"up": "dn", "dn": "up", "lf": "rt", "rt": "lf"}
    SIDES = ("up", "dn", "lf", "rt")

    barrier = pltpu.get_barrier_semaphore()
    for who in SIDES:
        @pl.when(has[who])
        def _():
            pl.semaphore_signal(barrier, inc=1, device_id=targets[who], device_id_type=MESH_ID)

    def clear(refs):
        for ref in refs:
            ref[...] = jnp.zeros_like(ref)

    for who, refs in (("up", (ru_e, ru_l, ru_a, ru_b)), ("dn", (rd_e, rd_l, rd_a, rd_b)),
                      ("lf", (rl_e, rl_l, rl_a, rl_b)), ("rt", (rr_e, rr_l, rr_a, rr_b))):
        @pl.when(jnp.logical_not(has[who]))
        def _():
            clear(refs)

    def fetch(src, dst, base, rows, sem):
        out = []
        for t in range(2):
            out.append(pltpu.make_async_copy(
                src.at[:, pl.ds(128 * t, 128)], dst.at[pl.ds(t * base[1] + base[0], rows), :], in_sem.at[sem, t]))
        for copy in out:
            copy.start()
        return out

    pad = (PAD, PR)
    cp_dep = fetch(dep_hbm, dbuf, (0, ROWS), ROWS, 0)
    cp_mx = fetch(mx_hbm, mbuf, pad, FLAT - ROWS, 1)
    cp_se = fetch(se_hbm, sbuf, pad, FLAT, 2)
    cp_tr = fetch(tr_hbm, cbuf, pad, FLAT, 3)
    cp_ns = fetch(ns_hbm, ybuf, pad, FLAT, 4)
    cp_es = fetch(es_hbm, xbuf, pad, FLAT, 5)

    def wait_all(copies):
        for copy in copies:
            copy.wait()

    row16 = lax.broadcasted_iota(jnp.int32, (16, 128), 0)
    lane16 = lax.broadcasted_iota(jnp.int32, (16, 128), 1)
    lane8 = lax.broadcasted_iota(jnp.int32, (8, 128), 1)
    levrow = row16.astype(F32)
    slot = lane8 // 4
    part = lane8 % 4
    levlane = (lane8 // 8).astype(F32)

    def get(ref, t, lev, shift=0):
        return ref[pl.ds(t * PR + PAD + 16 * lev + shift, 16), :]

    def put(ref, t, lev, value):
        ref[pl.ds(t * PR + PAD + 16 * lev, 16), :] = value

    def row_of(ref, t, r):
        return ref[pl.ds(t * PR + PAD + r, LEV, stride=ROWS), :]

    def row_add(ref, t, r, value):
        where = pl.ds(t * PR + PAD + r, LEV, stride=ROWS)
        ref[where, :] = ref[where, :] + value

    zero_pad = jnp.zeros((8, 128), F32)
    for ref in (cbuf, gbuf, ebuf, g2buf):
        for t in range(2):
            ref[pl.ds(t * PR, PAD), :] = zero_pad
            ref[pl.ds(t * PR + PAD + FLAT, PAD), :] = zero_pad

    def pack_tiles(read):
        acc = jnp.zeros((8, 128), F32)
        for k in range(32):
            left, right = read(k)
            merged = jnp.where(lane8 < 64, left, right)
            acc = jnp.where(slot == k, roll(merged, 4 * k + 2, 1), acc)
        return acc

    def pack(ref):
        return pack_tiles(lambda k: (
            ref[pl.ds(PAD + 8 * k, 8), :], ref[pl.ds(PR + PAD + 8 * k, 8), :]))

    wait_all(cp_dep)
    wait_all(cp_mx)
    dep = [dbuf[pl.ds(16 * t, 16), :].astype(F32) for t in range(2)]
    dm_y = [jnp.where(row16 == 0, 0.0, jnp.minimum(dep[t], roll(dep[t], 1, 0))) for t in range(2)]
    dr = [roll(dep[t], 1, 1) for t in range(2)]
    dm_x = [jnp.where(lane16 == 0, 0.0, jnp.minimum(dep[0], dr[0])),
            jnp.minimum(dep[1], jnp.where(lane16 == 0, dr[0], dr[1]))]
    dp = jnp.zeros((8, 128), F32)
    for k in range(2):
        merged = jnp.where(lane8 < 64, dep[0][8 * k:8 * k + 8], dep[1][8 * k:8 * k + 8])
        dp = jnp.where(slot == k, roll(merged, 4 * k + 2, 1), dp)
    for width in (8, 16, 32, 64):
        dp = dp + roll(dp, width, 1)
    for t in range(2):
        dn_e[pl.ds(64 + 8 * t, 8), :] = jnp.broadcast_to(dep[t][15:16, :], (8, 128))
        up_e[pl.ds(96 + 8 * t, 8), :] = jnp.broadcast_to(dep[t][0:1, :], (8, 128))

    above = [None, None]
    fprev = [None, None]
    for lev in range(LEV):
        for t in range(2):
            if lev < LEV - 1:
                below = jnp.where(dep[t] > lev + 1.0, get(mbuf, t, lev), 0.0)
            else:
                below = jnp.zeros((16, 128), F32)
            if lev == 0:
                pivot = 1.0 + below
            else:
                pivot = (1.0 + below) + above[t] * (1.0 - fprev[t])
            inv = 1.0 / pivot
            put(ibuf, t, lev, inv)
            if lev > 0:
                put(hbuf, t, lev, above[t] * inv)
            above[t] = below
            fprev[t] = below * inv
            put(fbuf, t, lev, fprev[t])

    def backward(ref, last, finish, out_ref):
        cur = last
        for t in range(2):
            put(out_ref, t, LEV - 1, finish(t, LEV - 1, cur[t]))
        for lev in range(LEV - 2, -1, -1):
            for t in range(2):
                cur[t] = get(ref, t, lev) + get(fbuf, t, lev) * cur[t]
                put(out_ref, t, lev, finish(t, lev, cur[t]))

    def forward(read, ref):
        cur = [None, None]
        for lev in range(LEV):
            rhs = read(lev)
            for t in range(2):
                value = rhs[t] * get(ibuf, t, lev)
                if lev > 0:
                    value = value + get(hbuf, t, lev) * cur[t]
                cur[t] = value
                put(ref, t, lev, value)
        return cur

    def masked(t, lev, value):
        return jnp.where(dep[t] > lev, value, 0.0)

    wait_all(cp_se)
    last = forward(lambda lev: [get(sbuf, t, lev) for t in range(2)], qbuf)
    backward(qbuf, last, masked, gbuf)

    wait_all(cp_tr)
    wait_all(cp_ns)
    wait_all(cp_es)
    c_rows = {r: [row_of(cbuf, t, r) for t in range(2)] for r in (0, 1, 14, 15)}
    s_rows = {r: [row_of(ybuf, t, r) for t in range(2)] for r in (0, 1, 15)}
    d_rows = {r: [jnp.broadcast_to(dep[t][r:r + 1, :], (16, 128)) for t in range(2)] for r in (0, 1, 14, 15)}
    for t in range(2):
        dn_e[pl.ds(16 * t, 16), :] = c_rows[14][t]
        dn_e[pl.ds(32 + 16 * t, 16), :] = c_rows[15][t]
        up_e[pl.ds(16 * t, 16), :] = c_rows[0][t]
        up_e[pl.ds(32 + 16 * t, 16), :] = c_rows[1][t]
        up_e[pl.ds(64 + 16 * t, 16), :] = s_rows[0][t]
    c_pk = pack(cbuf)
    s_pk = pack(xbuf)
    px_e[pl.ds(0, 8), :] = c_pk
    px_e[pl.ds(8, 8), :] = s_pk
    px_e[pl.ds(16, 8), :] = dp

    a1 = [jnp.where(jnp.minimum(d_rows[0][t], d_rows[1][t]) > levrow, s_rows[1][t], 0.0) for t in range(2)]
    a15 = [jnp.where(jnp.minimum(d_rows[14][t], d_rows[15][t]) > levrow, s_rows[15][t], 0.0) for t in range(2)]
    a_pk = jnp.where(jnp.minimum(dp, roll(dp, 1, 1)) > levlane, s_pk, 0.0)

    def edge_rows(ref):
        return {r: [row_of(ref, t, r) for t in range(2)] for r in (0, 1, 14, 15)}

    def stage_gradient(ref, dn, up, px):
        rows = edge_rows(ref)
        for t in range(2):
            dn[pl.ds(16 * t, 16), :] = rows[15][t]
            dn[pl.ds(32 + 16 * t, 16), :] = a15[t] * (rows[15][t] - rows[14][t])
            up[pl.ds(16 * t, 16), :] = rows[0][t]
            up[pl.ds(32 + 16 * t, 16), :] = a1[t] * (rows[1][t] - rows[0][t])
        packed = pack(ref)
        px[pl.ds(0, 8), :] = packed
        px[pl.ds(8, 8), :] = a_pk * (packed - roll(packed, 1, 1))
        return rows, packed

    g_rows, g_pk = stage_gradient(gbuf, dn_l, up_l, px_l)

    def message(index, srcs, dsts):
        copies = {}
        for d, who in enumerate(("up", "dn", "lf", "rt")):
            copies[who] = pltpu.make_async_remote_copy(
                src_ref=srcs[who], dst_ref=dsts[who],
                send_sem=send_sem.at[index, d], recv_sem=recv_sem.at[index, d],
                device_id=targets[who], device_id_type=MESH_ID)
        for who in SIDES:
            @pl.when(has[who])
            def _():
                copies[who].start()
        return copies

    pl.semaphore_wait(barrier, sum(has[who].astype(jnp.int32) for who in SIDES))
    msg_e = message(0, {"up": up_e, "dn": dn_e, "lf": px_e, "rt": px_e},
                    {"up": rd_e, "dn": ru_e, "lf": rr_e, "rt": rl_e})
    msg_l = message(1, {"up": up_l, "dn": dn_l, "lf": px_l, "rt": px_l},
                    {"up": rd_l, "dn": ru_l, "lf": rr_l, "rt": rl_l})

    def arrive(copies):
        for who in ("lf", "rt", "up", "dn"):
            @pl.when(has[opposite[who]])
            def _():
                copies[who].wait_recv()

    lane0 = lane16 == 0
    lane127 = lane16 == 127
    lane_lo2 = lane16 < 2
    lane_hi2 = lane16 >= 126
    row0 = row16 == 0
    row15 = row16 == 15
    row_lo2 = row16 < 2
    row_hi2 = row16 >= 14

    def explicit_level(src, lev, dst):
        level = lax.convert_element_type(lev, F32) if not isinstance(lev, int) else float(lev)
        c = [get(src, t, lev) for t in range(2)]
        r1 = [roll(c[t], 1, 1) for t in range(2)]
        r2 = [roll(c[t], 2, 1) for t in range(2)]
        q1 = [roll(c[t], 127, 1) for t in range(2)]
        m1 = [r1[0], jnp.where(lane0, r1[0], r1[1])]
        m2 = [jnp.where(lane_lo2, 0.0, r2[0]), jnp.where(lane_lo2, r2[0], r2[1])]
        p1 = [jnp.where(lane127, q1[1], q1[0]), jnp.where(lane127, 0.0, q1[1])]
        gx = [jnp.where(dm_x[t] > level,
                        get(xbuf, t, lev) * (7.0 * (c[t] + m1[t]) - (p1[t] + m2[t])) - 1.2 * (c[t] - m1[t]), 0.0)
              for t in range(2)]
        h1 = [roll(gx[t], 127, 1) for t in range(2)]
        gxp = [jnp.where(lane127, h1[1], h1[0]), jnp.where(lane127, h1[0], h1[1])]
        for t in range(2):
            ym1 = get(src, t, lev, -1)
            ym2 = jnp.where(row_lo2, 0.0, get(src, t, lev, -2))
            yp1 = jnp.where(row15, 0.0, get(src, t, lev, 1))
            gy = jnp.where(dm_y[t] > level,
                           get(ybuf, t, lev) * (7.0 * (c[t] + ym1) - (yp1 + ym2)) - 1.2 * (c[t] - ym1), 0.0)
            gyp = roll(gy, 15, 0)
            put(dst, t, lev, c[t] * (1.0 - 0.2 * c[t]) + ((gx[t] - gxp[t]) + (gy - gyp)) * TWELFTH)

    def adjoint_level(src, lev, dst, extra):
        level = lax.convert_element_type(lev, F32) if not isinstance(lev, int) else float(lev)
        g = [get(src, t, lev) for t in range(2)]
        r1 = [roll(g[t], 1, 1) for t in range(2)]
        m1 = [r1[0], jnp.where(lane0, r1[0], r1[1])]
        j = [jnp.where(dm_x[t] > level, g[t] - m1[t], 0.0) for t in range(2)]
        cx = [get(xbuf, t, lev) * j[t] for t in range(2)]
        u = [7.0 * cx[t] + 1.2 * j[t] for t in range(2)]
        w = [7.0 * cx[t] - 1.2 * j[t] for t in range(2)]
        u1 = [roll(u[t], 127, 1) for t in range(2)]
        up1 = [jnp.where(lane127, u1[1], u1[0]), jnp.where(lane127, 0.0, u1[1])]
        k1 = [roll(cx[t], 1, 1) for t in range(2)]
        cm1 = [jnp.where(lane0, 0.0, k1[0]), jnp.where(lane0, k1[0], k1[1])]
        k2 = [roll(cx[t], 126, 1) for t in range(2)]
        cp2 = [jnp.where(lane_hi2, k2[1], k2[0]), jnp.where(lane_hi2, 0.0, k2[1])]
        for t in range(2):
            jy = jnp.where(dm_y[t] > level, g[t] - get(src, t, lev, -1), 0.0)
            cy = get(ybuf, t, lev) * jy
            uy = 7.0 * cy + 1.2 * jy
            wy = 7.0 * cy - 1.2 * jy
            uyp = roll(uy, 15, 0)
            cym = jnp.where(row0, 0.0, roll(cy, 1, 0))
            cyp = jnp.where(row_hi2, 0.0, roll(cy, 14, 0))
            total = ((w[t] + up1[t]) - (cm1[t] + cp2[t])) + ((wy + uyp) - (cym + cyp))
            put(dst, t, lev, extra(t, lev, g[t]) + total * TWELFTH)

    def over_levels(body):
        if UNROLL == LEV:
            for lev in range(LEV):
                body(lev)
            return

        def step(i, carry):
            for u in range(UNROLL):
                body(i * UNROLL + u)
            return carry
        lax.fori_loop(0, LEV // UNROLL, step, 0)

    over_levels(lambda lev: explicit_level(cbuf, lev, ebuf))
    over_levels(lambda lev: adjoint_level(gbuf, lev, rbuf, lambda t, l, g: g))

    arrive(msg_e)
    du = [jnp.concatenate([ru_e[pl.ds(64 + 8 * t, 8), :]] * 2, axis=0) for t in range(2)]
    dd = [jnp.concatenate([rd_e[pl.ds(96 + 8 * t, 8), :]] * 2, axis=0) for t in range(2)]
    open0 = [jnp.minimum(du[t], d_rows[0][t]) > levrow for t in range(2)]
    openn = [jnp.minimum(dd[t], d_rows[15][t]) > levrow for t in range(2)]
    a0 = [jnp.where(open0[t], s_rows[0][t], 0.0) for t in range(2)]
    an = [jnp.where(openn[t], rd_e[pl.ds(64 + 16 * t, 16), :], 0.0) for t in range(2)]
    b0 = [jnp.where(open0[t], 1.2, 0.0) for t in range(2)]
    bn = [jnp.where(openn[t], 1.2, 0.0) for t in range(2)]
    is2 = part == 2
    low = part < 2
    sp_l = rl_e[pl.ds(8, 8), :]
    sp_r = rr_e[pl.ds(8, 8), :]
    dp_l = rl_e[pl.ds(16, 8), :]
    dp_r = rr_e[pl.ds(16, 8), :]
    d_near = jnp.where(low, roll(dp_r, -1, 1), roll(dp_l, 1, 1))
    open_pk = jnp.minimum(dp, d_near) > levlane
    af_pk = jnp.where(open_pk, jnp.where(low, roll(sp_r, -1, 1), s_pk), 0.0)
    bf_pk = jnp.where(open_pk, 1.2, 0.0)
    a_next = roll(a_pk, -1, 1)

    def explicit_rows(ref, rows, ru, rd):
        for t in range(2):
            c2 = ru[pl.ds(16 * t, 16), :]
            c1 = ru[pl.ds(32 + 16 * t, 16), :]
            n0 = rd[pl.ds(16 * t, 16), :]
            n1 = rd[pl.ds(32 + 16 * t, 16), :]
            r0, r1, r14, r15 = (rows[r][t] for r in (0, 1, 14, 15))
            g0 = a0[t] * (7.0 * (r0 + c1) - (r1 + c2)) - b0[t] * (r0 - c1)
            gn = an[t] * (7.0 * (n0 + r15) - (n1 + r14)) - bn[t] * (n0 - r15)
            p = a1[t] * c1
            q = a15[t] * n0
            row_add(ref, t, 0, (g0 + p) * TWELFTH)
            row_add(ref, t, 1, p * -TWELFTH)
            row_add(ref, t, 14, q * TWELFTH)
            row_add(ref, t, 15, (q + gn) * -TWELFTH)

    def explicit_cols(c, rl, rr):
        cl = rl[pl.ds(0, 8), :]
        cr = rr[pl.ds(0, 8), :]
        x1, x2 = roll(cl, 1, 1), roll(cl, 2, 1)
        y1, y2 = roll(cr, -1, 1), roll(cr, -2, 1)
        near = jnp.where(low, y1, x1)
        far = jnp.where(low, y2 + roll(c, 1, 1), x2 + roll(c, -1, 1))
        step = jnp.where(low, y1 - c, c - x1)
        face = af_pk * (7.0 * (c + near) - far) - bf_pk * step
        return TWELFTH * jnp.where(
            part == 0, a_next * y2,
            jnp.where(part == 1, -(a_pk * y1 + face),
                      jnp.where(part == 2, face + a_next * x1, -(a_pk * x2))))

    def adjoint_rows(ref, rows, ru, rd):
        for t in range(2):
            gu = ru[pl.ds(16 * t, 16), :]
            cu = ru[pl.ds(32 + 16 * t, 16), :]
            gd = rd[pl.ds(16 * t, 16), :]
            cd = rd[pl.ds(32 + 16 * t, 16), :]
            j0 = rows[0][t] - gu
            jn = gd - rows[15][t]
            f0 = a0[t] * j0
            fn = an[t] * jn
            row_add(ref, t, 0, (7.0 * f0 - cu - b0[t] * j0) * TWELFTH)
            row_add(ref, t, 1, f0 * -TWELFTH)
            row_add(ref, t, 14, fn * -TWELFTH)
            row_add(ref, t, 15, (7.0 * fn - cd + bn[t] * jn) * TWELFTH)

    def adjoint_cols(g, rl, rr):
        gl = rl[pl.ds(0, 8), :]
        kl = rl[pl.ds(8, 8), :]
        gr = rr[pl.ds(0, 8), :]
        kr = rr[pl.ds(8, 8), :]
        j = jnp.where(low, roll(gr, -1, 1) - g, g - roll(gl, 1, 1))
        f = af_pk * j
        s = bf_pk * j
        outer = jnp.where(low, roll(kr, -2, 1), roll(kl, 1, 1))
        edge = 7.0 * f - outer + jnp.where(low, s, -s)
        inner = -jnp.where(low, roll(f, -1, 1), roll(f, 1, 1))
        return TWELFTH * jnp.where((part == 1) | is2, edge, inner)

    lane_lo2_8 = lane8 < 2
    lane_hi2_8 = lane8 >= 126

    def with_cols(ref, packed, lev):
        halves = [roll(packed, 126 - 4 * (2 * lev + k), 1) for k in range(2)]
        left = jnp.concatenate([jnp.where(lane_lo2_8, h, 0.0) for h in halves], axis=0)
        right = jnp.concatenate([jnp.where(lane_hi2_8, h, 0.0) for h in halves], axis=0)
        return [get(ref, 0, lev) + left, get(ref, 1, lev) + right]

    def solve_explicit(packed, out_ref):
        def read(lev):
            both = with_cols(ebuf, packed, lev)
            return [masked(t, lev, both[t]) for t in range(2)]
        last = forward(read, qbuf)
        backward(qbuf, last, lambda t, lev, v: v, out_ref)

    explicit_rows(ebuf, c_rows, ru_e, rd_e)
    solve_explicit(explicit_cols(c_pk, rl_e, rr_e), sbuf)

    f_rows = edge_rows(sbuf)
    f_pk = pack(sbuf)
    for t in range(2):
        dn_a[pl.ds(16 * t, 16), :] = f_rows[14][t]
        dn_a[pl.ds(32 + 16 * t, 16), :] = f_rows[15][t]
        up_a[pl.ds(16 * t, 16), :] = f_rows[0][t]
        up_a[pl.ds(32 + 16 * t, 16), :] = f_rows[1][t]
    px_a[...] = f_pk
    msg_a = message(2, {"up": up_a, "dn": dn_a, "lf": px_a, "rt": px_a},
                    {"up": rd_a, "dn": ru_a, "lf": rr_a, "rt": rl_a})

    arrive(msg_l)
    adjoint_rows(rbuf, g_rows, ru_l, rd_l)
    packed = adjoint_cols(g_pk, rl_l, rr_l)

    def read_adjoint(lev):
        both = with_cols(rbuf, packed, lev)
        return [both[t] - 0.4 * get(sbuf, t, lev) * get(gbuf, t, lev) for t in range(2)]

    last = forward(read_adjoint, qbuf)
    backward(qbuf, last, masked, g2buf)
    h_rows, h_pk = stage_gradient(g2buf, dn_b, up_b, px_b)
    msg_b = message(3, {"up": up_b, "dn": dn_b, "lf": px_b, "rt": px_b},
                    {"up": rd_b, "dn": ru_b, "lf": rr_b, "rt": rl_b})

    over_levels(lambda lev: explicit_level(sbuf, lev, ebuf))
    over_levels(lambda lev: adjoint_level(
        g2buf, lev, rbuf, lambda t, l, g: g * (1.0 - 0.4 * get(cbuf, t, l))))

    arrive(msg_a)
    explicit_rows(ebuf, f_rows, ru_a, rd_a)
    solve_explicit(explicit_cols(f_pk, rl_a, rr_a), final)

    arrive(msg_b)
    adjoint_rows(rbuf, h_rows, ru_b, rd_b)
    packed_b = adjoint_cols(h_pk, rl_b, rr_b)
    for lev in range(LEV):
        both = with_cols(rbuf, packed_b, lev)
        for t in range(2):
            put(rbuf, t, lev, both[t])

    for msg in (msg_e, msg_l, msg_a, msg_b):
        for who in SIDES:
            @pl.when(has[who])
            def _():
                msg[who].wait_send()


def flush_kernel(final, adjoint, fin_hbm, adj_hbm, sem):
    copies = []
    for n, (src, dst) in enumerate(((final, fin_hbm), (adjoint, adj_hbm))):
        for t in range(2):
            copies.append(pltpu.make_async_copy(
                src.at[pl.ds(t * PR + PAD, FLAT), :], dst.at[:, pl.ds(128 * t, 128)], sem.at[n, t]))
    for copy in copies:
        copy.start()
    for copy in copies:
        copy.wait()


def solution(mesh):
    n_group, n_tile = mesh.shape["group"], mesh.shape["tile"]

    def shards(tracer, east_speed, north_speed, mixing, depth_levels, sensitivity):
        lev, rows, cols = tracer.shape

        def flat(x):
            return x.reshape(-1, cols)

        def vm(n):
            return pltpu.VMEM((n, 128), F32)

        big = 2 * PR
        hbm = pl.BlockSpec(memory_space=pltpu.HBM)
        vmem = pl.BlockSpec(memory_space=pltpu.VMEM)
        out = pl.pallas_call(
            functools.partial(kernel, n_group, n_tile),
            out_shape=[jax.ShapeDtypeStruct((big, 128), F32)] * 2,
            in_specs=[hbm] * 6,
            out_specs=[vmem] * 2,
            scratch_shapes=(
                [vm(big)] * 9 + [pltpu.VMEM((32, 128), jnp.int32)] + [vm(big)] * 3
                + [vm(80), vm(112), vm(64), vm(64), vm(64), vm(64), vm(64), vm(64)]
                + [vm(24), vm(16), vm(8), vm(16)]
                + [vm(80), vm(112), vm(64), vm(64), vm(64), vm(64), vm(64), vm(64)]
                + [vm(24), vm(24), vm(16), vm(16), vm(8), vm(8), vm(16), vm(16)]
                + [pltpu.SemaphoreType.DMA((6, 2)),
                   pltpu.SemaphoreType.DMA((4, 4)), pltpu.SemaphoreType.DMA((4, 4))]
            ),
            compiler_params=pltpu.CompilerParams(collective_id=0, has_side_effects=True, vmem_limit_bytes=VMEM_MAIN),
        )(*[pltpu.with_memory_space_constraint(x, pltpu.HBM) for x in (
            flat(tracer), flat(east_speed), flat(north_speed), flat(mixing), depth_levels, flat(sensitivity))])
        out = pl.pallas_call(
            flush_kernel,
            out_shape=[jax.ShapeDtypeStruct((lev * rows, cols), F32)] * 2,
            in_specs=[vmem] * 2,
            out_specs=[hbm] * 2,
            scratch_shapes=[pltpu.SemaphoreType.DMA((2, 2))],
            compiler_params=pltpu.CompilerParams(vmem_limit_bytes=VMEM_FLUSH),
        )(*out)
        return tuple(o.reshape(lev, rows, cols) for o in out)

    spec = P(None, "group", "tile")
    return jax.shard_map(
        shards, mesh=mesh, in_specs=(spec, spec, spec, spec, P("group", "tile"), spec),
        out_specs=(spec, spec), check_vma=False)
```

```python
import functools

import jax
import jax.numpy as jnp
from jax import lax
from jax.experimental import pallas as pl
from jax.experimental.pallas import tpu as pltpu
from jax.sharding import PartitionSpec as P

F32 = jnp.float32
MESH_ID = pl.DeviceIdType.MESH
LEV = 16
ROWS = 16
FLAT = LEV * ROWS
PAD = 8
PR = FLAT + 2 * PAD
TWELFTH = 1.0 / 12.0
UNROLL = 16
VMEM_MAIN = 32 * 2**20
VMEM_FLUSH = 8 * 2**20


def roll(x, shift, axis):
    n = x.shape[axis]
    return pltpu.roll(x, shift % n, axis)


def kernel(
    n_group, n_tile,
    tr_hbm, es_hbm, ns_hbm, mx_hbm, dep_hbm, se_hbm,
    final, rbuf,
    cbuf, ebuf, xbuf, ybuf, mbuf, gbuf, fbuf, hbuf, ibuf, dbuf, sbuf, g2buf, qbuf,
    dn_e, up_e, dn_l, up_l, dn_a, up_a, dn_b, up_b, px_e, px_l, px_a, px_b,
    ru_e, rd_e, ru_l, rd_l, ru_a, rd_a, ru_b, rd_b,
    rl_e, rr_e, rl_l, rr_l, rl_a, rr_a, rl_b, rr_b,
    in_sem, send_sem, recv_sem,
):
    gi = lax.axis_index("group")
    ti = lax.axis_index("tile")
    up_id = lax.rem(gi + n_group - 1, n_group)
    dn_id = lax.rem(gi + 1, n_group)
    lf_id = lax.rem(ti + n_tile - 1, n_tile)
    rt_id = lax.rem(ti + 1, n_tile)
    targets = {"up": (up_id, ti), "dn": (dn_id, ti), "lf": (gi, lf_id), "rt": (gi, rt_id)}

    has = {"up": gi > 0, "dn": gi < n_group - 1, "lf": ti > 0, "rt": ti < n_tile - 1}
    opposite = {"up": "dn", "dn": "up", "lf": "rt", "rt": "lf"}
    SIDES = ("up", "dn", "lf", "rt")

    barrier = pltpu.get_barrier_semaphore()
    for who in SIDES:
        @pl.when(has[who])
        def _():
            pl.semaphore_signal(barrier, inc=1, device_id=targets[who], device_id_type=MESH_ID)

    def clear(refs):
        for ref in refs:
            ref[...] = jnp.zeros_like(ref)

    for who, refs in (("up", (ru_e, ru_l, ru_a, ru_b)), ("dn", (rd_e, rd_l, rd_a, rd_b)),
                      ("lf", (rl_e, rl_l, rl_a, rl_b)), ("rt", (rr_e, rr_l, rr_a, rr_b))):
        @pl.when(jnp.logical_not(has[who]))
        def _():
            clear(refs)

    def fetch(src, dst, base, rows, sem):
        out = []
        for t in range(2):
            out.append(pltpu.make_async_copy(
                src.at[:, pl.ds(128 * t, 128)], dst.at[pl.ds(t * base[1] + base[0], rows), :], in_sem.at[sem, t]))
        for copy in out:
            copy.start()
        return out

    pad = (PAD, PR)
    cp_dep = fetch(dep_hbm, dbuf, (0, ROWS), ROWS, 0)
    cp_tr = fetch(tr_hbm, cbuf, pad, FLAT, 3)
    cp_ns = fetch(ns_hbm, ybuf, pad, FLAT, 4)
    cp_es = fetch(es_hbm, xbuf, pad, FLAT, 5)
    cp_mx = fetch(mx_hbm, mbuf, pad, FLAT - ROWS, 1)
    cp_se = fetch(se_hbm, sbuf, pad, FLAT, 2)

    def wait_all(copies):
        for copy in copies:
            copy.wait()

    row16 = lax.broadcasted_iota(jnp.int32, (16, 128), 0)
    lane16 = lax.broadcasted_iota(jnp.int32, (16, 128), 1)
    lane8 = lax.broadcasted_iota(jnp.int32, (8, 128), 1)
    levrow = row16.astype(F32)
    slot = lane8 // 4
    part = lane8 % 4
    levlane = (lane8 // 8).astype(F32)

    def get(ref, t, lev, shift=0):
        return ref[pl.ds(t * PR + PAD + 16 * lev + shift, 16), :]

    def put(ref, t, lev, value):
        ref[pl.ds(t * PR + PAD + 16 * lev, 16), :] = value

    def row_of(ref, t, r):
        return ref[pl.ds(t * PR + PAD + r, LEV, stride=ROWS), :]

    def row_add(ref, t, r, value):
        where = pl.ds(t * PR + PAD + r, LEV, stride=ROWS)
        ref[where, :] = ref[where, :] + value

    zero_pad = jnp.zeros((8, 128), F32)
    for ref in (cbuf, gbuf, ebuf, g2buf):
        for t in range(2):
            ref[pl.ds(t * PR, PAD), :] = zero_pad
            ref[pl.ds(t * PR + PAD + FLAT, PAD), :] = zero_pad

    def pack_tiles(read):
        acc = jnp.zeros((8, 128), F32)
        for k in range(32):
            left, right = read(k)
            merged = jnp.where(lane8 < 64, left, right)
            acc = jnp.where(slot == k, roll(merged, 4 * k + 2, 1), acc)
        return acc

    def pack(ref):
        return pack_tiles(lambda k: (
            ref[pl.ds(PAD + 8 * k, 8), :], ref[pl.ds(PR + PAD + 8 * k, 8), :]))

    def message(index, srcs, dsts):
        copies = {}
        for d, who in enumerate(SIDES):
            copies[who] = pltpu.make_async_remote_copy(
                src_ref=srcs[who], dst_ref=dsts[who],
                send_sem=send_sem.at[index, d], recv_sem=recv_sem.at[index, d],
                device_id=targets[who], device_id_type=MESH_ID)
        return copies

    def start(copies, sides):
        for who in sides:
            @pl.when(has[who])
            def _():
                copies[who].start()

    def arrive(copies, sides):
        for who in sides:
            @pl.when(has[opposite[who]])
            def _():
                copies[who].wait_recv()

    COLS = ("lf", "rt")
    LINES = ("up", "dn")
    msg_e = message(0, {"up": up_e, "dn": dn_e, "lf": px_e, "rt": px_e},
                    {"up": rd_e, "dn": ru_e, "lf": rr_e, "rt": rl_e})
    msg_l = message(1, {"up": up_l, "dn": dn_l, "lf": px_l, "rt": px_l},
                    {"up": rd_l, "dn": ru_l, "lf": rr_l, "rt": rl_l})
    msg_a = message(2, {"up": up_a, "dn": dn_a, "lf": px_a, "rt": px_a},
                    {"up": rd_a, "dn": ru_a, "lf": rr_a, "rt": rl_a})
    msg_b = message(3, {"up": up_b, "dn": dn_b, "lf": px_b, "rt": px_b},
                    {"up": rd_b, "dn": ru_b, "lf": rr_b, "rt": rl_b})

    def edge_rows(ref):
        return {r: [row_of(ref, t, r) for t in range(2)] for r in (0, 1, 14, 15)}

    def send_gradient(ref, dn, up, px, msg):
        rows = edge_rows(ref)
        for t in range(2):
            dn[pl.ds(16 * t, 16), :] = rows[15][t]
            dn[pl.ds(32 + 16 * t, 16), :] = a15[t] * (rows[15][t] - rows[14][t])
            up[pl.ds(16 * t, 16), :] = rows[0][t]
            up[pl.ds(32 + 16 * t, 16), :] = a1[t] * (rows[1][t] - rows[0][t])
        start(msg, LINES)
        packed = pack(ref)
        px[pl.ds(0, 8), :] = packed
        px[pl.ds(8, 8), :] = a_pk * (packed - roll(packed, 1, 1))
        start(msg, COLS)
        return rows, packed

    wait_all(cp_dep)
    wait_all(cp_tr)
    wait_all(cp_ns)
    dep = [dbuf[pl.ds(16 * t, 16), :].astype(F32) for t in range(2)]
    c_rows = edge_rows(cbuf)
    s_rows = {r: [row_of(ybuf, t, r) for t in range(2)] for r in (0, 1, 15)}
    d_rows = {r: [jnp.broadcast_to(dep[t][r:r + 1, :], (16, 128)) for t in range(2)] for r in (0, 1, 14, 15)}
    for t in range(2):
        dn_e[pl.ds(16 * t, 16), :] = c_rows[14][t]
        dn_e[pl.ds(32 + 16 * t, 16), :] = c_rows[15][t]
        up_e[pl.ds(16 * t, 16), :] = c_rows[0][t]
        up_e[pl.ds(32 + 16 * t, 16), :] = c_rows[1][t]
        up_e[pl.ds(64 + 16 * t, 16), :] = s_rows[0][t]
    row8 = lax.broadcasted_iota(jnp.int32, (8, 128), 0)
    dn_e[pl.ds(64, 8), :] = jnp.where(row8 == 0, d_rows[15][0][:8], d_rows[15][1][:8])
    up_e[pl.ds(96, 8), :] = jnp.where(row8 == 0, d_rows[0][0][:8], d_rows[0][1][:8])
    pl.semaphore_wait(barrier, sum(has[who].astype(jnp.int32) for who in SIDES))
    start(msg_e, LINES)

    wait_all(cp_es)
    dm_y = [jnp.where(row16 == 0, 0.0, jnp.minimum(dep[t], roll(dep[t], 1, 0))) for t in range(2)]
    dr = [roll(dep[t], 1, 1) for t in range(2)]
    dm_x = [jnp.where(lane16 == 0, 0.0, jnp.minimum(dep[0], dr[0])),
            jnp.minimum(dep[1], jnp.where(lane16 == 0, dr[0], dr[1]))]
    dp = jnp.zeros((8, 128), F32)
    for k in range(2):
        merged = jnp.where(lane8 < 64, dep[0][8 * k:8 * k + 8], dep[1][8 * k:8 * k + 8])
        dp = jnp.where(slot == k, roll(merged, 4 * k + 2, 1), dp)
    for width in (8, 16, 32, 64):
        dp = dp + roll(dp, width, 1)
    c_pk = pack(cbuf)
    s_pk = pack(xbuf)
    px_e[pl.ds(0, 8), :] = c_pk
    px_e[pl.ds(8, 8), :] = s_pk
    px_e[pl.ds(16, 8), :] = dp
    start(msg_e, COLS)

    a1 = [jnp.where(jnp.minimum(d_rows[0][t], d_rows[1][t]) > levrow, s_rows[1][t], 0.0) for t in range(2)]
    a15 = [jnp.where(jnp.minimum(d_rows[14][t], d_rows[15][t]) > levrow, s_rows[15][t], 0.0) for t in range(2)]
    a_pk = jnp.where(jnp.minimum(dp, roll(dp, 1, 1)) > levlane, s_pk, 0.0)

    wait_all(cp_mx)
    above = [None, None]
    fprev = [None, None]
    for lev in range(LEV):
        for t in range(2):
            if lev < LEV - 1:
                below = jnp.where(dep[t] > lev + 1.0, get(mbuf, t, lev), 0.0)
            else:
                below = jnp.zeros((16, 128), F32)
            if lev == 0:
                pivot = 1.0 + below
            else:
                pivot = (1.0 + below) + above[t] * (1.0 - fprev[t])
            inv = 1.0 / pivot
            put(ibuf, t, lev, inv)
            if lev > 0:
                put(hbuf, t, lev, above[t] * inv)
            above[t] = below
            fprev[t] = below * inv
            put(fbuf, t, lev, fprev[t])

    def backward(ref, last, finish, out_ref):
        cur = last
        for t in range(2):
            put(out_ref, t, LEV - 1, finish(t, LEV - 1, cur[t]))
        for lev in range(LEV - 2, -1, -1):
            for t in range(2):
                cur[t] = get(ref, t, lev) + get(fbuf, t, lev) * cur[t]
                put(out_ref, t, lev, finish(t, lev, cur[t]))

    def forward(read, ref):
        cur = [None, None]
        for lev in range(LEV):
            rhs = read(lev)
            for t in range(2):
                value = rhs[t] * get(ibuf, t, lev)
                if lev > 0:
                    value = value + get(hbuf, t, lev) * cur[t]
                cur[t] = value
                put(ref, t, lev, value)
        return cur

    def masked(t, lev, value):
        return jnp.where(dep[t] > lev, value, 0.0)

    wait_all(cp_se)
    last = forward(lambda lev: [get(sbuf, t, lev) for t in range(2)], qbuf)
    backward(qbuf, last, masked, gbuf)
    g_rows, g_pk = send_gradient(gbuf, dn_l, up_l, px_l, msg_l)

    lane0 = lane16 == 0
    lane127 = lane16 == 127
    lane_lo2 = lane16 < 2
    lane_hi2 = lane16 >= 126
    row0 = row16 == 0
    row15 = row16 == 15
    row_lo2 = row16 < 2
    row_hi2 = row16 >= 14

    def explicit_level(src, lev, dst):
        level = lax.convert_element_type(lev, F32) if not isinstance(lev, int) else float(lev)
        c = [get(src, t, lev) for t in range(2)]
        r1 = [roll(c[t], 1, 1) for t in range(2)]
        r2 = [roll(c[t], 2, 1) for t in range(2)]
        q1 = [roll(c[t], 127, 1) for t in range(2)]
        m1 = [r1[0], jnp.where(lane0, r1[0], r1[1])]
        m2 = [jnp.where(lane_lo2, 0.0, r2[0]), jnp.where(lane_lo2, r2[0], r2[1])]
        p1 = [jnp.where(lane127, q1[1], q1[0]), jnp.where(lane127, 0.0, q1[1])]
        gx = [jnp.where(dm_x[t] > level,
                        get(xbuf, t, lev) * (7.0 * (c[t] + m1[t]) - (p1[t] + m2[t])) - 1.2 * (c[t] - m1[t]), 0.0)
              for t in range(2)]
        h1 = [roll(gx[t], 127, 1) for t in range(2)]
        gxp = [jnp.where(lane127, h1[1], h1[0]), jnp.where(lane127, h1[0], h1[1])]
        for t in range(2):
            ym1 = get(src, t, lev, -1)
            ym2 = jnp.where(row_lo2, 0.0, get(src, t, lev, -2))
            yp1 = jnp.where(row15, 0.0, get(src, t, lev, 1))
            gy = jnp.where(dm_y[t] > level,
                           get(ybuf, t, lev) * (7.0 * (c[t] + ym1) - (yp1 + ym2)) - 1.2 * (c[t] - ym1), 0.0)
            gyp = roll(gy, 15, 0)
            put(dst, t, lev, c[t] * (1.0 - 0.2 * c[t]) + ((gx[t] - gxp[t]) + (gy - gyp)) * TWELFTH)

    def adjoint_level(src, lev, dst, extra):
        level = lax.convert_element_type(lev, F32) if not isinstance(lev, int) else float(lev)
        g = [get(src, t, lev) for t in range(2)]
        r1 = [roll(g[t], 1, 1) for t in range(2)]
        m1 = [r1[0], jnp.where(lane0, r1[0], r1[1])]
        j = [jnp.where(dm_x[t] > level, g[t] - m1[t], 0.0) for t in range(2)]
        cx = [get(xbuf, t, lev) * j[t] for t in range(2)]
        u = [7.0 * cx[t] + 1.2 * j[t] for t in range(2)]
        w = [7.0 * cx[t] - 1.2 * j[t] for t in range(2)]
        u1 = [roll(u[t], 127, 1) for t in range(2)]
        up1 = [jnp.where(lane127, u1[1], u1[0]), jnp.where(lane127, 0.0, u1[1])]
        k1 = [roll(cx[t], 1, 1) for t in range(2)]
        cm1 = [jnp.where(lane0, 0.0, k1[0]), jnp.where(lane0, k1[0], k1[1])]
        k2 = [roll(cx[t], 126, 1) for t in range(2)]
        cp2 = [jnp.where(lane_hi2, k2[1], k2[0]), jnp.where(lane_hi2, 0.0, k2[1])]
        for t in range(2):
            jy = jnp.where(dm_y[t] > level, g[t] - get(src, t, lev, -1), 0.0)
            cy = get(ybuf, t, lev) * jy
            uy = 7.0 * cy + 1.2 * jy
            wy = 7.0 * cy - 1.2 * jy
            uyp = roll(uy, 15, 0)
            cym = jnp.where(row0, 0.0, roll(cy, 1, 0))
            cyp = jnp.where(row_hi2, 0.0, roll(cy, 14, 0))
            total = ((w[t] + up1[t]) - (cm1[t] + cp2[t])) + ((wy + uyp) - (cym + cyp))
            put(dst, t, lev, extra(t, lev, g[t]) + total * TWELFTH)

    def over_levels(body):
        if UNROLL == LEV:
            for lev in range(LEV):
                body(lev)
            return

        def step(i, carry):
            for u in range(UNROLL):
                body(i * UNROLL + u)
            return carry
        lax.fori_loop(0, LEV // UNROLL, step, 0)

    over_levels(lambda lev: explicit_level(cbuf, lev, ebuf))
    over_levels(lambda lev: adjoint_level(gbuf, lev, rbuf, lambda t, l, g: g))

    arrive(msg_e, COLS)
    is2 = part == 2
    low = part < 2
    sp_l = rl_e[pl.ds(8, 8), :]
    sp_r = rr_e[pl.ds(8, 8), :]
    dp_l = rl_e[pl.ds(16, 8), :]
    dp_r = rr_e[pl.ds(16, 8), :]
    d_near = jnp.where(low, roll(dp_r, -1, 1), roll(dp_l, 1, 1))
    open_pk = jnp.minimum(dp, d_near) > levlane
    af_pk = jnp.where(open_pk, jnp.where(low, roll(sp_r, -1, 1), s_pk), 0.0)
    bf_pk = jnp.where(open_pk, 1.2, 0.0)
    a_next = roll(a_pk, -1, 1)

    def explicit_rows(ref, rows, ru, rd):
        for t in range(2):
            c2 = ru[pl.ds(16 * t, 16), :]
            c1 = ru[pl.ds(32 + 16 * t, 16), :]
            n0 = rd[pl.ds(16 * t, 16), :]
            n1 = rd[pl.ds(32 + 16 * t, 16), :]
            r0, r1, r14, r15 = (rows[r][t] for r in (0, 1, 14, 15))
            g0 = a0[t] * (7.0 * (r0 + c1) - (r1 + c2)) - b0[t] * (r0 - c1)
            gn = an[t] * (7.0 * (n0 + r15) - (n1 + r14)) - bn[t] * (n0 - r15)
            p = a1[t] * c1
            q = a15[t] * n0
            row_add(ref, t, 0, (g0 + p) * TWELFTH)
            row_add(ref, t, 1, p * -TWELFTH)
            row_add(ref, t, 14, q * TWELFTH)
            row_add(ref, t, 15, (q + gn) * -TWELFTH)

    def explicit_cols(c, rl, rr):
        cl = rl[pl.ds(0, 8), :]
        cr = rr[pl.ds(0, 8), :]
        x1, x2 = roll(cl, 1, 1), roll(cl, 2, 1)
        y1, y2 = roll(cr, -1, 1), roll(cr, -2, 1)
        near = jnp.where(low, y1, x1)
        far = jnp.where(low, y2 + roll(c, 1, 1), x2 + roll(c, -1, 1))
        step = jnp.where(low, y1 - c, c - x1)
        face = af_pk * (7.0 * (c + near) - far) - bf_pk * step
        return TWELFTH * jnp.where(
            part == 0, a_next * y2,
            jnp.where(part == 1, -(a_pk * y1 + face),
                      jnp.where(part == 2, face + a_next * x1, -(a_pk * x2))))

    def adjoint_rows(ref, rows, ru, rd):
        for t in range(2):
            gu = ru[pl.ds(16 * t, 16), :]
            cu = ru[pl.ds(32 + 16 * t, 16), :]
            gd = rd[pl.ds(16 * t, 16), :]
            cd = rd[pl.ds(32 + 16 * t, 16), :]
            j0 = rows[0][t] - gu
            jn = gd - rows[15][t]
            f0 = a0[t] * j0
            fn = an[t] * jn
            row_add(ref, t, 0, (7.0 * f0 - cu - b0[t] * j0) * TWELFTH)
            row_add(ref, t, 1, f0 * -TWELFTH)
            row_add(ref, t, 14, fn * -TWELFTH)
            row_add(ref, t, 15, (7.0 * fn - cd + bn[t] * jn) * TWELFTH)

    def adjoint_cols(g, rl, rr):
        gl = rl[pl.ds(0, 8), :]
        kl = rl[pl.ds(8, 8), :]
        gr = rr[pl.ds(0, 8), :]
        kr = rr[pl.ds(8, 8), :]
        j = jnp.where(low, roll(gr, -1, 1) - g, g - roll(gl, 1, 1))
        f = af_pk * j
        s = bf_pk * j
        outer = jnp.where(low, roll(kr, -2, 1), roll(kl, 1, 1))
        edge = 7.0 * f - outer + jnp.where(low, s, -s)
        inner = -jnp.where(low, roll(f, -1, 1), roll(f, 1, 1))
        return TWELFTH * jnp.where((part == 1) | is2, edge, inner)

    lane_lo2_8 = lane8 < 2
    lane_hi2_8 = lane8 >= 126

    def add_cols(ref, packed, extra):
        for lev in range(LEV):
            both = with_cols(ref, packed, lev)
            for t in range(2):
                put(ref, t, lev, extra(t, lev, both[t]))

    def with_cols(ref, packed, lev):
        halves = [roll(packed, 126 - 4 * (2 * lev + k), 1) for k in range(2)]
        left = jnp.concatenate([jnp.where(lane_lo2_8, h, 0.0) for h in halves], axis=0)
        right = jnp.concatenate([jnp.where(lane_hi2_8, h, 0.0) for h in halves], axis=0)
        return [get(ref, 0, lev) + left, get(ref, 1, lev) + right]

    def plain(t, lev, value):
        return value

    def solve_explicit(out_ref):
        last = forward(lambda lev: [masked(t, lev, get(ebuf, t, lev)) for t in range(2)], qbuf)
        backward(qbuf, last, plain, out_ref)

    add_cols(ebuf, explicit_cols(c_pk, rl_e, rr_e), plain)
    arrive(msg_e, LINES)
    du = [jnp.broadcast_to(ru_e[pl.ds(64 + t, 1), :], (16, 128)) for t in range(2)]
    dd = [jnp.broadcast_to(rd_e[pl.ds(96 + t, 1), :], (16, 128)) for t in range(2)]
    open0 = [jnp.minimum(du[t], d_rows[0][t]) > levrow for t in range(2)]
    openn = [jnp.minimum(dd[t], d_rows[15][t]) > levrow for t in range(2)]
    a0 = [jnp.where(open0[t], s_rows[0][t], 0.0) for t in range(2)]
    an = [jnp.where(openn[t], rd_e[pl.ds(64 + 16 * t, 16), :], 0.0) for t in range(2)]
    b0 = [jnp.where(open0[t], 1.2, 0.0) for t in range(2)]
    bn = [jnp.where(openn[t], 1.2, 0.0) for t in range(2)]
    explicit_rows(ebuf, c_rows, ru_e, rd_e)
    solve_explicit(sbuf)

    f_rows = edge_rows(sbuf)
    for t in range(2):
        dn_a[pl.ds(16 * t, 16), :] = f_rows[14][t]
        dn_a[pl.ds(32 + 16 * t, 16), :] = f_rows[15][t]
        up_a[pl.ds(16 * t, 16), :] = f_rows[0][t]
        up_a[pl.ds(32 + 16 * t, 16), :] = f_rows[1][t]
    start(msg_a, LINES)
    f_pk = pack(sbuf)
    px_a[...] = f_pk
    start(msg_a, COLS)

    arrive(msg_l, COLS)
    add_cols(rbuf, adjoint_cols(g_pk, rl_l, rr_l),
             lambda t, lev, v: v - 0.4 * get(sbuf, t, lev) * get(gbuf, t, lev))
    arrive(msg_l, LINES)
    adjoint_rows(rbuf, g_rows, ru_l, rd_l)
    last = forward(lambda lev: [get(rbuf, t, lev) for t in range(2)], qbuf)
    backward(qbuf, last, masked, g2buf)
    h_rows, h_pk = send_gradient(g2buf, dn_b, up_b, px_b, msg_b)

    over_levels(lambda lev: explicit_level(sbuf, lev, ebuf))
    over_levels(lambda lev: adjoint_level(
        g2buf, lev, rbuf, lambda t, l, g: g * (1.0 - 0.4 * get(cbuf, t, l))))

    arrive(msg_a, COLS)
    add_cols(ebuf, explicit_cols(f_pk, rl_a, rr_a), plain)
    arrive(msg_a, LINES)
    explicit_rows(ebuf, f_rows, ru_a, rd_a)
    solve_explicit(final)

    arrive(msg_b, COLS)
    add_cols(rbuf, adjoint_cols(h_pk, rl_b, rr_b), plain)
    arrive(msg_b, LINES)
    adjoint_rows(rbuf, h_rows, ru_b, rd_b)

    for msg in (msg_e, msg_l, msg_a, msg_b):
        for who in SIDES:
            @pl.when(has[who])
            def _():
                msg[who].wait_send()


def flush_kernel(final, adjoint, fin_hbm, adj_hbm, sem):
    copies = []
    for n, (src, dst) in enumerate(((final, fin_hbm), (adjoint, adj_hbm))):
        for t in range(2):
            copies.append(pltpu.make_async_copy(
                src.at[pl.ds(t * PR + PAD, FLAT), :], dst.at[:, pl.ds(128 * t, 128)], sem.at[n, t]))
    for copy in copies:
        copy.start()
    for copy in copies:
        copy.wait()


def solution(mesh):
    n_group, n_tile = mesh.shape["group"], mesh.shape["tile"]

    def shards(tracer, east_speed, north_speed, mixing, depth_levels, sensitivity):
        lev, rows, cols = tracer.shape

        def flat(x):
            return x.reshape(-1, cols)

        def vm(n):
            return pltpu.VMEM((n, 128), F32)

        big = 2 * PR
        hbm = pl.BlockSpec(memory_space=pltpu.HBM)
        vmem = pl.BlockSpec(memory_space=pltpu.VMEM)
        out = pl.pallas_call(
            functools.partial(kernel, n_group, n_tile),
            out_shape=[jax.ShapeDtypeStruct((big, 128), F32)] * 2,
            in_specs=[hbm] * 6,
            out_specs=[vmem] * 2,
            scratch_shapes=(
                [vm(big)] * 9 + [pltpu.VMEM((32, 128), jnp.int32)] + [vm(big)] * 3
                + [vm(72), vm(104), vm(64), vm(64), vm(64), vm(64), vm(64), vm(64)]
                + [vm(24), vm(16), vm(8), vm(16)]
                + [vm(72), vm(104), vm(64), vm(64), vm(64), vm(64), vm(64), vm(64)]
                + [vm(24), vm(24), vm(16), vm(16), vm(8), vm(8), vm(16), vm(16)]
                + [pltpu.SemaphoreType.DMA((6, 2)),
                   pltpu.SemaphoreType.DMA((4, 4)), pltpu.SemaphoreType.DMA((4, 4))]
            ),
            compiler_params=pltpu.CompilerParams(collective_id=0, has_side_effects=True, vmem_limit_bytes=VMEM_MAIN),
        )(*[pltpu.with_memory_space_constraint(x, pltpu.HBM) for x in (
            flat(tracer), flat(east_speed), flat(north_speed), flat(mixing), depth_levels, flat(sensitivity))])
        out = pl.pallas_call(
            flush_kernel,
            out_shape=[jax.ShapeDtypeStruct((lev * rows, cols), F32)] * 2,
            in_specs=[vmem] * 2,
            out_specs=[hbm] * 2,
            scratch_shapes=[pltpu.SemaphoreType.DMA((2, 2))],
            compiler_params=pltpu.CompilerParams(vmem_limit_bytes=VMEM_FLUSH),
        )(*out)
        return tuple(o.reshape(lev, rows, cols) for o in out)

    spec = P(None, "group", "tile")
    return jax.shard_map(
        shards, mesh=mesh, in_specs=(spec, spec, spec, spec, P("group", "tile"), spec),
        out_specs=(spec, spec), check_vma=False)
```

```python
import functools

import jax
import jax.numpy as jnp
from jax import lax
from jax.experimental import pallas as pl
from jax.experimental.pallas import tpu as pltpu
from jax.sharding import PartitionSpec as P

F32 = jnp.float32
MESH_ID = pl.DeviceIdType.MESH
LEV = 16
ROWS = 16
FLAT = LEV * ROWS
PAD = 8
PR = FLAT + 2 * PAD
TWELFTH = 1.0 / 12.0
CHUNK = 8
VMEM_MAIN = 32 * 2**20
VMEM_FLUSH = 8 * 2**20


def roll(x, shift, axis):
    n = x.shape[axis]
    return pltpu.roll(x, shift % n, axis)


def kernel(
    n_group, n_tile,
    tr_hbm, es_hbm, ns_hbm, mx_hbm, dep_hbm, se_hbm,
    final, rbuf,
    cbuf, ebuf, xbuf, ybuf, mbuf, gbuf, fbuf, hbuf, ibuf, dbuf, sbuf, g2buf, qbuf,
    dn_e, up_e, dn_l, up_l, dn_a, up_a, dn_b, up_b, px_e, px_l, px_a, px_b,
    ru_e, rd_e, ru_l, rd_l, ru_a, rd_a, ru_b, rd_b,
    rl_e, rr_e, rl_l, rr_l, rl_a, rr_a, rl_b, rr_b,
    stencils, in_sem, send_sem, recv_sem,
):
    gi = lax.axis_index("group")
    ti = lax.axis_index("tile")
    up_id = lax.rem(gi + n_group - 1, n_group)
    dn_id = lax.rem(gi + 1, n_group)
    lf_id = lax.rem(ti + n_tile - 1, n_tile)
    rt_id = lax.rem(ti + 1, n_tile)
    targets = {"up": (up_id, ti), "dn": (dn_id, ti), "lf": (gi, lf_id), "rt": (gi, rt_id)}

    has = {"up": gi > 0, "dn": gi < n_group - 1, "lf": ti > 0, "rt": ti < n_tile - 1}
    opposite = {"up": "dn", "dn": "up", "lf": "rt", "rt": "lf"}
    SIDES = ("up", "dn", "lf", "rt")

    barrier = pltpu.get_barrier_semaphore()
    for who in SIDES:
        @pl.when(has[who])
        def _():
            pl.semaphore_signal(barrier, inc=1, device_id=targets[who], device_id_type=MESH_ID)

    def clear(refs):
        for ref in refs:
            ref[...] = jnp.zeros_like(ref)

    for who, refs in (("up", (ru_e, ru_l, ru_a, ru_b)), ("dn", (rd_e, rd_l, rd_a, rd_b)),
                      ("lf", (rl_e, rl_l, rl_a, rl_b)), ("rt", (rr_e, rr_l, rr_a, rr_b))):
        @pl.when(jnp.logical_not(has[who]))
        def _():
            clear(refs)

    def fetch(src, dst, base, rows, sem):
        out = []
        for t in range(2):
            out.append(pltpu.make_async_copy(
                src.at[:, pl.ds(128 * t, 128)], dst.at[pl.ds(t * base[1] + base[0], rows), :], in_sem.at[sem, t]))
        for copy in out:
            copy.start()
        return out

    pad = (PAD, PR)
    cp_dep = fetch(dep_hbm, dbuf, (0, ROWS), ROWS, 0)
    cp_tr = fetch(tr_hbm, cbuf, pad, FLAT, 3)
    cp_ns = fetch(ns_hbm, ybuf, pad, FLAT, 4)
    cp_es = fetch(es_hbm, xbuf, pad, FLAT, 5)
    cp_mx = fetch(mx_hbm, mbuf, pad, FLAT - ROWS, 1)
    cp_se = fetch(se_hbm, sbuf, pad, FLAT, 2)

    def wait_all(copies):
        for copy in copies:
            copy.wait()

    row16 = lax.broadcasted_iota(jnp.int32, (16, 128), 0)
    lane16 = lax.broadcasted_iota(jnp.int32, (16, 128), 1)
    lane8 = lax.broadcasted_iota(jnp.int32, (8, 128), 1)
    levrow = row16.astype(F32)
    slot = lane8 // 4
    part = lane8 % 4
    levlane = (lane8 // 8).astype(F32)

    def get(ref, t, lev, shift=0):
        return ref[pl.ds(t * PR + PAD + 16 * lev + shift, 16), :]

    def put(ref, t, lev, value):
        ref[pl.ds(t * PR + PAD + 16 * lev, 16), :] = value

    def row_of(ref, t, r):
        return ref[pl.ds(t * PR + PAD + r, LEV, stride=ROWS), :]

    def row_put(ref, t, r, value):
        ref[pl.ds(t * PR + PAD + r, LEV, stride=ROWS), :] = value

    zero_pad = jnp.zeros((8, 128), F32)
    for ref in (cbuf, gbuf, ebuf, g2buf):
        for t in range(2):
            ref[pl.ds(t * PR, PAD), :] = zero_pad
            ref[pl.ds(t * PR + PAD + FLAT, PAD), :] = zero_pad

    def pack_tiles(read):
        acc = jnp.zeros((8, 128), F32)
        for k in range(32):
            left, right = read(k)
            merged = jnp.where(lane8 < 64, left, right)
            acc = jnp.where(slot == k, roll(merged, 4 * k + 2, 1), acc)
        return acc

    def pack(ref):
        return pack_tiles(lambda k: (
            ref[pl.ds(PAD + 8 * k, 8), :], ref[pl.ds(PR + PAD + 8 * k, 8), :]))

    def message(index, srcs, dsts):
        copies = {}
        for d, who in enumerate(SIDES):
            copies[who] = pltpu.make_async_remote_copy(
                src_ref=srcs[who], dst_ref=dsts[who],
                send_sem=send_sem.at[index, d], recv_sem=recv_sem.at[index, d],
                device_id=targets[who], device_id_type=MESH_ID)
        return copies

    def start(copies, sides):
        for who in sides:
            @pl.when(has[who])
            def _():
                copies[who].start()

    def arrive(copies, sides):
        for who in sides:
            @pl.when(has[opposite[who]])
            def _():
                copies[who].wait_recv()

    COLS = ("lf", "rt")
    LINES = ("up", "dn")
    msg_e = message(0, {"up": up_e, "dn": dn_e, "lf": px_e, "rt": px_e},
                    {"up": rd_e, "dn": ru_e, "lf": rr_e, "rt": rl_e})
    msg_l = message(1, {"up": up_l, "dn": dn_l, "lf": px_l, "rt": px_l},
                    {"up": rd_l, "dn": ru_l, "lf": rr_l, "rt": rl_l})
    msg_a = message(2, {"up": up_a, "dn": dn_a, "lf": px_a, "rt": px_a},
                    {"up": rd_a, "dn": ru_a, "lf": rr_a, "rt": rl_a})
    msg_b = message(3, {"up": up_b, "dn": dn_b, "lf": px_b, "rt": px_b},
                    {"up": rd_b, "dn": ru_b, "lf": rr_b, "rt": rl_b})

    def edge_rows(ref):
        return {r: [row_of(ref, t, r) for t in range(2)] for r in (0, 1, 14, 15)}

    def send_rows(ref, dn, up, msg):
        rows = edge_rows(ref)
        for t in range(2):
            dn[pl.ds(16 * t, 16), :] = rows[15][t]
            dn[pl.ds(32 + 16 * t, 16), :] = a15[t] * (rows[15][t] - rows[14][t])
            up[pl.ds(16 * t, 16), :] = rows[0][t]
            up[pl.ds(32 + 16 * t, 16), :] = a1[t] * (rows[1][t] - rows[0][t])
        start(msg, LINES)
        return rows

    def send_cols(ref, px, msg):
        packed = pack(ref)
        px[pl.ds(0, 8), :] = packed
        px[pl.ds(8, 8), :] = a_pk * (packed - roll(packed, 1, 1))
        start(msg, COLS)
        return packed

    offset = lax.broadcasted_iota(jnp.int32, (256, 256), 1) - lax.broadcasted_iota(jnp.int32, (256, 256), 0)
    for n, taps in enumerate((
        ((0, 7.0), (1, 7.0), (-1, -1.0), (2, -1.0)),
        ((0, 1.0), (1, -1.0)),
        ((0, 1.0), (-1, -1.0)),
        ((0, 7.0), (-1, 7.0), (1, -1.0), (-2, -1.0)),
    )):
        matrix = jnp.zeros((256, 256), F32)
        for shift, weight in taps:
            matrix = jnp.where(offset == shift, weight, matrix)
        stencils[:, pl.ds(256 * n, 256)] = matrix.astype(jnp.bfloat16)

    wait_all(cp_dep)
    wait_all(cp_tr)
    wait_all(cp_ns)
    dep = [dbuf[pl.ds(16 * t, 16), :].astype(F32) for t in range(2)]
    c_rows = edge_rows(cbuf)
    s_rows = {r: [row_of(ybuf, t, r) for t in range(2)] for r in (0, 1, 15)}
    d_rows = {r: [jnp.broadcast_to(dep[t][r:r + 1, :], (16, 128)) for t in range(2)] for r in (0, 1, 14, 15)}
    for t in range(2):
        dn_e[pl.ds(16 * t, 16), :] = c_rows[14][t]
        dn_e[pl.ds(32 + 16 * t, 16), :] = c_rows[15][t]
        up_e[pl.ds(16 * t, 16), :] = c_rows[0][t]
        up_e[pl.ds(32 + 16 * t, 16), :] = c_rows[1][t]
        up_e[pl.ds(64 + 16 * t, 16), :] = s_rows[0][t]
    row8 = lax.broadcasted_iota(jnp.int32, (8, 128), 0)
    dn_e[pl.ds(64, 8), :] = jnp.where(row8 == 0, d_rows[15][0][:8], d_rows[15][1][:8])
    up_e[pl.ds(96, 8), :] = jnp.where(row8 == 0, d_rows[0][0][:8], d_rows[0][1][:8])
    pl.semaphore_wait(barrier, sum(has[who].astype(jnp.int32) for who in SIDES))
    start(msg_e, LINES)

    wait_all(cp_es)
    dm_y = [jnp.where(row16 == 0, 0.0, jnp.minimum(dep[t], roll(dep[t], 1, 0))) for t in range(2)]
    dr = [roll(dep[t], 1, 1) for t in range(2)]
    dm_x = [jnp.where(lane16 == 0, 0.0, jnp.minimum(dep[0], dr[0])),
            jnp.minimum(dep[1], jnp.where(lane16 == 0, dr[0], dr[1]))]
    dp = jnp.zeros((8, 128), F32)
    for k in range(2):
        merged = jnp.where(lane8 < 64, dep[0][8 * k:8 * k + 8], dep[1][8 * k:8 * k + 8])
        dp = jnp.where(slot == k, roll(merged, 4 * k + 2, 1), dp)
    for width in (8, 16, 32, 64):
        dp = dp + roll(dp, width, 1)
    c_pk = pack(cbuf)
    s_pk = pack(xbuf)
    px_e[pl.ds(0, 8), :] = c_pk
    px_e[pl.ds(8, 8), :] = s_pk
    px_e[pl.ds(16, 8), :] = dp
    start(msg_e, COLS)

    a1 = [jnp.where(jnp.minimum(d_rows[0][t], d_rows[1][t]) > levrow, s_rows[1][t], 0.0) for t in range(2)]
    a15 = [jnp.where(jnp.minimum(d_rows[14][t], d_rows[15][t]) > levrow, s_rows[15][t], 0.0) for t in range(2)]
    a_pk = jnp.where(jnp.minimum(dp, roll(dp, 1, 1)) > levlane, s_pk, 0.0)

    wait_all(cp_mx)
    above = [None, None]
    fprev = [None, None]
    for lev in range(LEV):
        for t in range(2):
            if lev < LEV - 1:
                below = jnp.where(dep[t] > lev + 1.0, get(mbuf, t, lev), 0.0)
            else:
                below = jnp.zeros((16, 128), F32)
            if lev == 0:
                pivot = 1.0 + below
            else:
                pivot = (1.0 + below) + above[t] * (1.0 - fprev[t])
            inv = 1.0 / pivot
            put(ibuf, t, lev, inv)
            if lev > 0:
                put(hbuf, t, lev, above[t] * inv)
            above[t] = below
            fprev[t] = below * inv
            put(fbuf, t, lev, fprev[t])

    def backward(ref, last, finish, out_ref):
        cur = last
        for t in range(2):
            put(out_ref, t, LEV - 1, finish(t, LEV - 1, cur[t]))
        for lev in range(LEV - 2, -1, -1):
            for t in range(2):
                cur[t] = get(ref, t, lev) + get(fbuf, t, lev) * cur[t]
                put(out_ref, t, lev, finish(t, lev, cur[t]))

    def forward(read, ref):
        cur = [None, None]
        for lev in range(LEV):
            rhs = read(lev)
            for t in range(2):
                value = rhs[t] * get(ibuf, t, lev)
                if lev > 0:
                    value = value + get(hbuf, t, lev) * cur[t]
                cur[t] = value
                put(ref, t, lev, value)
        return cur

    def masked(t, lev, value):
        return jnp.where(dep[t] > lev, value, 0.0)

    wait_all(cp_se)
    last = forward(lambda lev: [get(sbuf, t, lev) for t in range(2)], qbuf)
    backward(qbuf, last, masked, gbuf)
    g_rows = send_rows(gbuf, dn_l, up_l, msg_l)
    g_pk = send_cols(gbuf, px_l, msg_l)

    lane0 = lane16 == 0
    lane127 = lane16 == 127
    lane_lo2 = lane16 < 2
    lane_hi2 = lane16 >= 126
    row0 = row16 == 0
    row15 = row16 == 15
    row_lo2 = row16 < 2
    row_hi2 = row16 >= 14

    def matmul(x, first, count):
        high = x.astype(jnp.bfloat16)
        low_part = (x - high.astype(F32)).astype(jnp.bfloat16)
        m = stencils[:, pl.ds(256 * first, 256 * count)]
        return (jnp.dot(high, m, preferred_element_type=F32)
                + jnp.dot(low_part, m, preferred_element_type=F32))

    def wide(ref, lev, count):
        return jnp.concatenate(
            [ref[pl.ds(t * PR + PAD + 16 * lev, 16 * count), :] for t in range(2)], axis=1)

    def open_faces(lev, count, value):
        rows = []
        for k in range(count):
            rows.append(jnp.concatenate(
                [jnp.where(dm_x[t] > float(lev + k), value[16 * k:16 * k + 16, 128 * t:128 * t + 128], 0.0)
                 for t in range(2)], axis=1))
        return jnp.concatenate(rows, axis=0)

    def explicit_levels(src, lev0, count, dst):
        td = matmul(wide(src, lev0, count), 0, 2)
        gx = open_faces(lev0, count, wide(xbuf, lev0, count) * td[:, :256] - 1.2 * td[:, 256:])
        ax = matmul(gx, 2, 1)
        for k in range(count):
            lev = lev0 + k
            for t in range(2):
                c = get(src, t, lev)
                ym1 = get(src, t, lev, -1)
                ym2 = jnp.where(row_lo2, 0.0, get(src, t, lev, -2))
                yp1 = jnp.where(row15, 0.0, get(src, t, lev, 1))
                gy = jnp.where(dm_y[t] > float(lev),
                               get(ybuf, t, lev) * (7.0 * (c + ym1) - (yp1 + ym2)) - 1.2 * (c - ym1), 0.0)
                gyp = roll(gy, 15, 0)
                put(dst, t, lev, c * (1.0 - 0.2 * c)
                    + (ax[16 * k:16 * k + 16, 128 * t:128 * t + 128] + (gy - gyp)) * TWELFTH)

    def adjoint_levels(src, lev0, count, dst, extra):
        j = open_faces(lev0, count, matmul(wide(src, lev0, count), 1, 1))
        ax = matmul(wide(xbuf, lev0, count) * j, 3, 1) - matmul(1.2 * j, 2, 1)
        for k in range(count):
            lev = lev0 + k
            for t in range(2):
                g = get(src, t, lev)
                jy = jnp.where(dm_y[t] > float(lev), g - get(src, t, lev, -1), 0.0)
                cy = get(ybuf, t, lev) * jy
                uy = 7.0 * cy + 1.2 * jy
                wy = 7.0 * cy - 1.2 * jy
                uyp = roll(uy, 15, 0)
                cym = jnp.where(row0, 0.0, roll(cy, 1, 0))
                cyp = jnp.where(row_hi2, 0.0, roll(cy, 14, 0))
                total = ax[16 * k:16 * k + 16, 128 * t:128 * t + 128] + ((wy + uyp) - (cym + cyp))
                put(dst, t, lev, extra(t, lev, g) + total * TWELFTH)

    def over_levels(body):
        for lev in range(0, LEV, CHUNK):
            body(lev)

    over_levels(lambda lev: explicit_levels(cbuf, lev, CHUNK, ebuf))
    over_levels(lambda lev: adjoint_levels(gbuf, lev, CHUNK, rbuf, lambda t, l, g: g))

    arrive(msg_e, COLS)
    is2 = part == 2
    low = part < 2
    sp_l = rl_e[pl.ds(8, 8), :]
    sp_r = rr_e[pl.ds(8, 8), :]
    dp_l = rl_e[pl.ds(16, 8), :]
    dp_r = rr_e[pl.ds(16, 8), :]
    d_near = jnp.where(low, roll(dp_r, -1, 1), roll(dp_l, 1, 1))
    open_pk = jnp.minimum(dp, d_near) > levlane
    af_pk = jnp.where(open_pk, jnp.where(low, roll(sp_r, -1, 1), s_pk), 0.0)
    bf_pk = jnp.where(open_pk, 1.2, 0.0)
    a_next = roll(a_pk, -1, 1)

    def explicit_rows(ref, base, rows, ru, rd):
        for t in range(2):
            c2 = ru[pl.ds(16 * t, 16), :]
            c1 = ru[pl.ds(32 + 16 * t, 16), :]
            n0 = rd[pl.ds(16 * t, 16), :]
            n1 = rd[pl.ds(32 + 16 * t, 16), :]
            r0, r1, r14, r15 = (rows[r][t] for r in (0, 1, 14, 15))
            g0 = a0[t] * (7.0 * (r0 + c1) - (r1 + c2)) - b0[t] * (r0 - c1)
            gn = an[t] * (7.0 * (n0 + r15) - (n1 + r14)) - bn[t] * (n0 - r15)
            p = a1[t] * c1
            q = a15[t] * n0
            row_put(ref, t, 0, base[0][t] + (g0 + p) * TWELFTH)
            row_put(ref, t, 1, base[1][t] + p * -TWELFTH)
            row_put(ref, t, 14, base[14][t] + q * TWELFTH)
            row_put(ref, t, 15, base[15][t] + (q + gn) * -TWELFTH)

    def explicit_cols(c, rl, rr):
        cl = rl[pl.ds(0, 8), :]
        cr = rr[pl.ds(0, 8), :]
        x1, x2 = roll(cl, 1, 1), roll(cl, 2, 1)
        y1, y2 = roll(cr, -1, 1), roll(cr, -2, 1)
        near = jnp.where(low, y1, x1)
        far = jnp.where(low, y2 + roll(c, 1, 1), x2 + roll(c, -1, 1))
        step = jnp.where(low, y1 - c, c - x1)
        face = af_pk * (7.0 * (c + near) - far) - bf_pk * step
        return TWELFTH * jnp.where(
            part == 0, a_next * y2,
            jnp.where(part == 1, -(a_pk * y1 + face),
                      jnp.where(part == 2, face + a_next * x1, -(a_pk * x2))))

    def adjoint_rows(ref, base, rows, ru, rd):
        for t in range(2):
            gu = ru[pl.ds(16 * t, 16), :]
            cu = ru[pl.ds(32 + 16 * t, 16), :]
            gd = rd[pl.ds(16 * t, 16), :]
            cd = rd[pl.ds(32 + 16 * t, 16), :]
            j0 = rows[0][t] - gu
            jn = gd - rows[15][t]
            f0 = a0[t] * j0
            fn = an[t] * jn
            row_put(ref, t, 0, base[0][t] + (7.0 * f0 - cu - b0[t] * j0) * TWELFTH)
            row_put(ref, t, 1, base[1][t] + f0 * -TWELFTH)
            row_put(ref, t, 14, base[14][t] + fn * -TWELFTH)
            row_put(ref, t, 15, base[15][t] + (7.0 * fn - cd + bn[t] * jn) * TWELFTH)

    def adjoint_cols(g, rl, rr):
        gl = rl[pl.ds(0, 8), :]
        kl = rl[pl.ds(8, 8), :]
        gr = rr[pl.ds(0, 8), :]
        kr = rr[pl.ds(8, 8), :]
        j = jnp.where(low, roll(gr, -1, 1) - g, g - roll(gl, 1, 1))
        f = af_pk * j
        s = bf_pk * j
        outer = jnp.where(low, roll(kr, -2, 1), roll(kl, 1, 1))
        edge = 7.0 * f - outer + jnp.where(low, s, -s)
        inner = -jnp.where(low, roll(f, -1, 1), roll(f, 1, 1))
        return TWELFTH * jnp.where((part == 1) | is2, edge, inner)

    lane_lo2_8 = lane8 < 2
    lane_hi2_8 = lane8 >= 126

    def add_cols(ref, packed, extra):
        for lev in range(LEV):
            both = with_cols(ref, packed, lev)
            for t in range(2):
                put(ref, t, lev, extra(t, lev, both[t]))

    def with_cols(ref, packed, lev):
        halves = [roll(packed, 126 - 4 * (2 * lev + k), 1) for k in range(2)]
        left = jnp.concatenate([jnp.where(lane_lo2_8, h, 0.0) for h in halves], axis=0)
        right = jnp.concatenate([jnp.where(lane_hi2_8, h, 0.0) for h in halves], axis=0)
        return [get(ref, 0, lev) + left, get(ref, 1, lev) + right]

    def plain(t, lev, value):
        return value

    def solve_explicit(out_ref):
        last = forward(lambda lev: [masked(t, lev, get(ebuf, t, lev)) for t in range(2)], qbuf)
        backward(qbuf, last, plain, out_ref)

    add_cols(ebuf, explicit_cols(c_pk, rl_e, rr_e), plain)
    base = edge_rows(ebuf)
    arrive(msg_e, LINES)
    du = [jnp.broadcast_to(ru_e[pl.ds(64 + t, 1), :], (16, 128)) for t in range(2)]
    dd = [jnp.broadcast_to(rd_e[pl.ds(96 + t, 1), :], (16, 128)) for t in range(2)]
    open0 = [jnp.minimum(du[t], d_rows[0][t]) > levrow for t in range(2)]
    openn = [jnp.minimum(dd[t], d_rows[15][t]) > levrow for t in range(2)]
    a0 = [jnp.where(open0[t], s_rows[0][t], 0.0) for t in range(2)]
    an = [jnp.where(openn[t], rd_e[pl.ds(64 + 16 * t, 16), :], 0.0) for t in range(2)]
    b0 = [jnp.where(open0[t], 1.2, 0.0) for t in range(2)]
    bn = [jnp.where(openn[t], 1.2, 0.0) for t in range(2)]
    explicit_rows(ebuf, base, c_rows, ru_e, rd_e)
    solve_explicit(sbuf)

    f_rows = edge_rows(sbuf)
    for t in range(2):
        dn_a[pl.ds(16 * t, 16), :] = f_rows[14][t]
        dn_a[pl.ds(32 + 16 * t, 16), :] = f_rows[15][t]
        up_a[pl.ds(16 * t, 16), :] = f_rows[0][t]
        up_a[pl.ds(32 + 16 * t, 16), :] = f_rows[1][t]
    start(msg_a, LINES)
    f_pk = pack(sbuf)
    px_a[...] = f_pk
    start(msg_a, COLS)

    arrive(msg_l, COLS)
    add_cols(rbuf, adjoint_cols(g_pk, rl_l, rr_l),
             lambda t, lev, v: v - 0.4 * get(sbuf, t, lev) * get(gbuf, t, lev))
    base = edge_rows(rbuf)
    arrive(msg_l, LINES)
    adjoint_rows(rbuf, base, g_rows, ru_l, rd_l)
    last = forward(lambda lev: [get(rbuf, t, lev) for t in range(2)], qbuf)
    backward(qbuf, last, masked, g2buf)
    h_rows = send_rows(g2buf, dn_b, up_b, msg_b)
    h_pk = send_cols(g2buf, px_b, msg_b)

    over_levels(lambda lev: explicit_levels(sbuf, lev, CHUNK, ebuf))
    over_levels(lambda lev: adjoint_levels(
        g2buf, lev, CHUNK, rbuf, lambda t, l, g: g * (1.0 - 0.4 * get(cbuf, t, l))))

    arrive(msg_a, COLS)
    add_cols(ebuf, explicit_cols(f_pk, rl_a, rr_a), plain)
    arrive(msg_b, COLS)
    add_cols(rbuf, adjoint_cols(h_pk, rl_b, rr_b), plain)
    base = edge_rows(ebuf)
    arrive(msg_a, LINES)
    explicit_rows(ebuf, base, f_rows, ru_a, rd_a)
    solve_explicit(final)

    base = edge_rows(rbuf)
    arrive(msg_b, LINES)
    adjoint_rows(rbuf, base, h_rows, ru_b, rd_b)

    for msg in (msg_e, msg_l, msg_a, msg_b):
        for who in SIDES:
            @pl.when(has[who])
            def _():
                msg[who].wait_send()


def flush_kernel(final, adjoint, fin_hbm, adj_hbm, sem):
    copies = []
    for n, (src, dst) in enumerate(((final, fin_hbm), (adjoint, adj_hbm))):
        for t in range(2):
            copies.append(pltpu.make_async_copy(
                src.at[pl.ds(t * PR + PAD, FLAT), :], dst.at[:, pl.ds(128 * t, 128)], sem.at[n, t]))
    for copy in copies:
        copy.start()
    for copy in copies:
        copy.wait()


def solution(mesh):
    n_group, n_tile = mesh.shape["group"], mesh.shape["tile"]

    def shards(tracer, east_speed, north_speed, mixing, depth_levels, sensitivity):
        lev, rows, cols = tracer.shape

        def flat(x):
            return x.reshape(-1, cols)

        def vm(n):
            return pltpu.VMEM((n, 128), F32)

        big = 2 * PR
        hbm = pl.BlockSpec(memory_space=pltpu.HBM)
        vmem = pl.BlockSpec(memory_space=pltpu.VMEM)
        out = pl.pallas_call(
            functools.partial(kernel, n_group, n_tile),
            out_shape=[jax.ShapeDtypeStruct((big, 128), F32)] * 2,
            in_specs=[hbm] * 6,
            out_specs=[vmem] * 2,
            scratch_shapes=(
                [vm(big)] * 9 + [pltpu.VMEM((32, 128), jnp.int32)] + [vm(big)] * 3
                + [vm(72), vm(104), vm(64), vm(64), vm(64), vm(64), vm(64), vm(64)]
                + [vm(24), vm(16), vm(8), vm(16)]
                + [vm(72), vm(104), vm(64), vm(64), vm(64), vm(64), vm(64), vm(64)]
                + [vm(24), vm(24), vm(16), vm(16), vm(8), vm(8), vm(16), vm(16)]
                + [pltpu.VMEM((256, 1024), jnp.bfloat16), pltpu.SemaphoreType.DMA((6, 2)),
                   pltpu.SemaphoreType.DMA((4, 4)), pltpu.SemaphoreType.DMA((4, 4))]
            ),
            compiler_params=pltpu.CompilerParams(collective_id=0, has_side_effects=True, vmem_limit_bytes=VMEM_MAIN),
        )(*[pltpu.with_memory_space_constraint(x, pltpu.HBM) for x in (
            flat(tracer), flat(east_speed), flat(north_speed), flat(mixing), depth_levels, flat(sensitivity))])
        out = pl.pallas_call(
            flush_kernel,
            out_shape=[jax.ShapeDtypeStruct((lev * rows, cols), F32)] * 2,
            in_specs=[vmem] * 2,
            out_specs=[hbm] * 2,
            scratch_shapes=[pltpu.SemaphoreType.DMA((2, 2))],
            compiler_params=pltpu.CompilerParams(vmem_limit_bytes=VMEM_FLUSH),
        )(*out)
        return tuple(o.reshape(lev, rows, cols) for o in out)

    spec = P(None, "group", "tile")
    return jax.shard_map(
        shards, mesh=mesh, in_specs=(spec, spec, spec, spec, P("group", "tile"), spec),
        out_specs=(spec, spec), check_vma=False)
```

```python
import functools

import jax
import jax.numpy as jnp
from jax import lax
from jax.experimental import pallas as pl
from jax.experimental.pallas import tpu as pltpu
from jax.sharding import PartitionSpec as P

F32 = jnp.float32
MESH_ID = pl.DeviceIdType.MESH
LEV = 16
ROWS = 16
FLAT = LEV * ROWS
PAD = 8
PR = FLAT + 2 * PAD
TWELFTH = 1.0 / 12.0
CHUNK = 8
VMEM_MAIN = 32 * 2**20
VMEM_FLUSH = 8 * 2**20


def roll(x, shift, axis):
    n = x.shape[axis]
    return pltpu.roll(x, shift % n, axis)


def kernel(
    n_group, n_tile,
    tr_hbm, es_hbm, ns_hbm, mx_hbm, dep_hbm, se_hbm,
    final, rbuf,
    cbuf, ebuf, xbuf, ybuf, mbuf, gbuf, fbuf, hbuf, ibuf, dbuf, sbuf, g2buf, qbuf,
    dn_e, up_e, dn_l, up_l, dn_a, up_a, dn_b, up_b, px_e, px_l, px_a, px_b,
    ru_e, rd_e, ru_l, rd_l, ru_a, rd_a, ru_b, rd_b,
    rl_e, rr_e, rl_l, rr_l, rl_a, rr_a, rl_b, rr_b,
    stencils, in_sem, send_sem, recv_sem,
):
    gi = lax.axis_index("group")
    ti = lax.axis_index("tile")
    up_id = lax.rem(gi + n_group - 1, n_group)
    dn_id = lax.rem(gi + 1, n_group)
    lf_id = lax.rem(ti + n_tile - 1, n_tile)
    rt_id = lax.rem(ti + 1, n_tile)
    targets = {"up": (up_id, ti), "dn": (dn_id, ti), "lf": (gi, lf_id), "rt": (gi, rt_id)}

    has = {"up": gi > 0, "dn": gi < n_group - 1, "lf": ti > 0, "rt": ti < n_tile - 1}
    opposite = {"up": "dn", "dn": "up", "lf": "rt", "rt": "lf"}
    SIDES = ("up", "dn", "lf", "rt")

    barrier = pltpu.get_barrier_semaphore()
    for who in SIDES:
        @pl.when(has[who])
        def _():
            pl.semaphore_signal(barrier, inc=1, device_id=targets[who], device_id_type=MESH_ID)

    def clear(refs):
        for ref in refs:
            ref[...] = jnp.zeros_like(ref)

    for who, refs in (("up", (ru_e, ru_l, ru_a, ru_b)), ("dn", (rd_e, rd_l, rd_a, rd_b)),
                      ("lf", (rl_e, rl_l, rl_a, rl_b)), ("rt", (rr_e, rr_l, rr_a, rr_b))):
        @pl.when(jnp.logical_not(has[who]))
        def _():
            clear(refs)

    def fetch(src, dst, base, rows, sem):
        out = []
        for t in range(2):
            out.append(pltpu.make_async_copy(
                src.at[:, pl.ds(128 * t, 128)], dst.at[pl.ds(t * base[1] + base[0], rows), :], in_sem.at[sem, t]))
        for copy in out:
            copy.start()
        return out

    pad = (PAD, PR)
    cp_dep = fetch(dep_hbm, dbuf, (0, ROWS), ROWS, 0)
    cp_tr = fetch(tr_hbm, cbuf, pad, FLAT, 3)
    cp_ns = fetch(ns_hbm, ybuf, pad, FLAT, 4)
    cp_es = fetch(es_hbm, xbuf, pad, FLAT, 5)
    cp_mx = fetch(mx_hbm, mbuf, pad, FLAT - ROWS, 1)
    cp_se = fetch(se_hbm, sbuf, pad, FLAT, 2)

    def wait_all(copies):
        for copy in copies:
            copy.wait()

    row16 = lax.broadcasted_iota(jnp.int32, (16, 128), 0)
    lane16 = lax.broadcasted_iota(jnp.int32, (16, 128), 1)
    lane8 = lax.broadcasted_iota(jnp.int32, (8, 128), 1)
    levrow = row16.astype(F32)
    slot = lane8 // 4
    part = lane8 % 4
    levlane = (lane8 // 8).astype(F32)

    def get(ref, t, lev, shift=0):
        return ref[pl.ds(t * PR + PAD + 16 * lev + shift, 16), :]

    def put(ref, t, lev, value):
        ref[pl.ds(t * PR + PAD + 16 * lev, 16), :] = value

    def row_of(ref, t, r):
        return ref[pl.ds(t * PR + PAD + r, LEV, stride=ROWS), :]

    def row_put(ref, t, r, value):
        ref[pl.ds(t * PR + PAD + r, LEV, stride=ROWS), :] = value

    zero_pad = jnp.zeros((8, 128), F32)
    for ref in (cbuf, gbuf, ebuf, g2buf):
        for t in range(2):
            ref[pl.ds(t * PR, PAD), :] = zero_pad
            ref[pl.ds(t * PR + PAD + FLAT, PAD), :] = zero_pad

    def pack_tiles(read):
        acc = jnp.zeros((8, 128), F32)
        for k in range(32):
            left, right = read(k)
            merged = jnp.where(lane8 < 64, left, right)
            acc = jnp.where(slot == k, roll(merged, 4 * k + 2, 1), acc)
        return acc

    def pack(ref):
        return pack_tiles(lambda k: (
            ref[pl.ds(PAD + 8 * k, 8), :], ref[pl.ds(PR + PAD + 8 * k, 8), :]))

    def message(index, srcs, dsts):
        copies = {}
        for d, who in enumerate(SIDES):
            copies[who] = pltpu.make_async_remote_copy(
                src_ref=srcs[who], dst_ref=dsts[who],
                send_sem=send_sem.at[index, d], recv_sem=recv_sem.at[index, d],
                device_id=targets[who], device_id_type=MESH_ID)
        return copies

    def start(copies, sides):
        for who in sides:
            @pl.when(has[who])
            def _():
                copies[who].start()

    def arrive(copies, sides):
        for who in sides:
            @pl.when(has[opposite[who]])
            def _():
                copies[who].wait_recv()

    COLS = ("lf", "rt")
    LINES = ("up", "dn")
    msg_e = message(0, {"up": up_e, "dn": dn_e, "lf": px_e, "rt": px_e},
                    {"up": rd_e, "dn": ru_e, "lf": rr_e, "rt": rl_e})
    msg_l = message(1, {"up": up_l, "dn": dn_l, "lf": px_l, "rt": px_l},
                    {"up": rd_l, "dn": ru_l, "lf": rr_l, "rt": rl_l})
    msg_a = message(2, {"up": up_a, "dn": dn_a, "lf": px_a, "rt": px_a},
                    {"up": rd_a, "dn": ru_a, "lf": rr_a, "rt": rl_a})
    msg_b = message(3, {"up": up_b, "dn": dn_b, "lf": px_b, "rt": px_b},
                    {"up": rd_b, "dn": ru_b, "lf": rr_b, "rt": rl_b})

    def edge_rows(ref):
        return {r: [row_of(ref, t, r) for t in range(2)] for r in (0, 1, 14, 15)}

    def send_rows(ref, dn, up, msg):
        rows = edge_rows(ref)
        for t in range(2):
            dn[pl.ds(16 * t, 16), :] = rows[15][t]
            dn[pl.ds(32 + 16 * t, 16), :] = a15[t] * (rows[15][t] - rows[14][t])
            up[pl.ds(16 * t, 16), :] = rows[0][t]
            up[pl.ds(32 + 16 * t, 16), :] = a1[t] * (rows[1][t] - rows[0][t])
        start(msg, LINES)
        return rows

    def send_cols(ref, px, msg):
        packed = pack(ref)
        px[pl.ds(0, 8), :] = packed
        px[pl.ds(8, 8), :] = a_pk * (packed - roll(packed, 1, 1))
        start(msg, COLS)
        return packed

    offset = lax.broadcasted_iota(jnp.int32, (256, 256), 1) - lax.broadcasted_iota(jnp.int32, (256, 256), 0)
    for n, taps in enumerate((
        ((0, 7.0), (1, 7.0), (-1, -1.0), (2, -1.0)),
        ((0, 1.0), (1, -1.0)),
        ((0, 1.0), (-1, -1.0)),
        ((0, 7.0), (-1, 7.0), (1, -1.0), (-2, -1.0)),
    )):
        matrix = jnp.zeros((256, 256), F32)
        for shift, weight in taps:
            matrix = jnp.where(offset == shift, weight, matrix)
        stencils[:, pl.ds(256 * n, 256)] = matrix.astype(jnp.bfloat16)

    wait_all(cp_dep)
    wait_all(cp_tr)
    wait_all(cp_ns)
    dep = [dbuf[pl.ds(16 * t, 16), :].astype(F32) for t in range(2)]
    c_rows = edge_rows(cbuf)
    s_rows = {r: [row_of(ybuf, t, r) for t in range(2)] for r in (0, 1, 15)}
    d_rows = {r: [jnp.broadcast_to(dep[t][r:r + 1, :], (16, 128)) for t in range(2)] for r in (0, 1, 14, 15)}
    for t in range(2):
        dn_e[pl.ds(16 * t, 16), :] = c_rows[14][t]
        dn_e[pl.ds(32 + 16 * t, 16), :] = c_rows[15][t]
        up_e[pl.ds(16 * t, 16), :] = c_rows[0][t]
        up_e[pl.ds(32 + 16 * t, 16), :] = c_rows[1][t]
        up_e[pl.ds(64 + 16 * t, 16), :] = s_rows[0][t]
    row8 = lax.broadcasted_iota(jnp.int32, (8, 128), 0)
    dn_e[pl.ds(64, 8), :] = jnp.where(row8 == 0, d_rows[15][0][:8], d_rows[15][1][:8])
    up_e[pl.ds(96, 8), :] = jnp.where(row8 == 0, d_rows[0][0][:8], d_rows[0][1][:8])
    pl.semaphore_wait(barrier, sum(has[who].astype(jnp.int32) for who in SIDES))
    start(msg_e, LINES)

    wait_all(cp_es)
    dm_y = [jnp.where(row16 == 0, 0.0, jnp.minimum(dep[t], roll(dep[t], 1, 0))) for t in range(2)]
    dr = [roll(dep[t], 1, 1) for t in range(2)]
    dm_x = [jnp.where(lane16 == 0, 0.0, jnp.minimum(dep[0], dr[0])),
            jnp.minimum(dep[1], jnp.where(lane16 == 0, dr[0], dr[1]))]
    dp = jnp.zeros((8, 128), F32)
    for k in range(2):
        merged = jnp.where(lane8 < 64, dep[0][8 * k:8 * k + 8], dep[1][8 * k:8 * k + 8])
        dp = jnp.where(slot == k, roll(merged, 4 * k + 2, 1), dp)
    for width in (8, 16, 32, 64):
        dp = dp + roll(dp, width, 1)
    c_pk = pack(cbuf)
    s_pk = pack(xbuf)
    px_e[pl.ds(0, 8), :] = c_pk
    px_e[pl.ds(8, 8), :] = s_pk
    px_e[pl.ds(16, 8), :] = dp
    start(msg_e, COLS)

    a1 = [jnp.where(jnp.minimum(d_rows[0][t], d_rows[1][t]) > levrow, s_rows[1][t], 0.0) for t in range(2)]
    a15 = [jnp.where(jnp.minimum(d_rows[14][t], d_rows[15][t]) > levrow, s_rows[15][t], 0.0) for t in range(2)]
    a_pk = jnp.where(jnp.minimum(dp, roll(dp, 1, 1)) > levlane, s_pk, 0.0)

    wait_all(cp_mx)
    above = [None, None]
    fprev = [None, None]
    for lev in range(LEV):
        for t in range(2):
            if lev < LEV - 1:
                below = jnp.where(dep[t] > lev + 1.0, get(mbuf, t, lev), 0.0)
            else:
                below = jnp.zeros((16, 128), F32)
            if lev == 0:
                pivot = 1.0 + below
            else:
                pivot = (1.0 + below) + above[t] * (1.0 - fprev[t])
            inv = 1.0 / pivot
            put(ibuf, t, lev, inv)
            if lev > 0:
                put(hbuf, t, lev, above[t] * inv)
            above[t] = below
            fprev[t] = below * inv
            put(fbuf, t, lev, fprev[t])

    def backward(ref, last, finish, out_ref):
        cur = last
        for t in range(2):
            put(out_ref, t, LEV - 1, finish(t, LEV - 1, cur[t]))
        for lev in range(LEV - 2, -1, -1):
            for t in range(2):
                cur[t] = get(ref, t, lev) + get(fbuf, t, lev) * cur[t]
                put(out_ref, t, lev, finish(t, lev, cur[t]))

    def forward(read, ref):
        cur = [None, None]
        for lev in range(LEV):
            rhs = read(lev)
            for t in range(2):
                value = rhs[t] * get(ibuf, t, lev)
                if lev > 0:
                    value = value + get(hbuf, t, lev) * cur[t]
                cur[t] = value
                put(ref, t, lev, value)
        return cur

    def masked(t, lev, value):
        return jnp.where(dep[t] > lev, value, 0.0)

    wait_all(cp_se)
    last = forward(lambda lev: [get(sbuf, t, lev) for t in range(2)], qbuf)
    backward(qbuf, last, masked, gbuf)
    g_rows = send_rows(gbuf, dn_l, up_l, msg_l)
    g_pk = send_cols(gbuf, px_l, msg_l)

    lane0 = lane16 == 0
    lane127 = lane16 == 127
    lane_lo2 = lane16 < 2
    lane_hi2 = lane16 >= 126
    row0 = row16 == 0
    row15 = row16 == 15
    row_lo2 = row16 < 2
    row_hi2 = row16 >= 14

    def matmul(x, first, count):
        high = x.astype(jnp.bfloat16)
        low_part = (x - high.astype(F32)).astype(jnp.bfloat16)
        m = stencils[:, pl.ds(256 * first, 256 * count)]
        return (jnp.dot(high, m, preferred_element_type=F32)
                + jnp.dot(low_part, m, preferred_element_type=F32))

    def wide(ref, lev, count):
        return jnp.concatenate(
            [ref[pl.ds(t * PR + PAD + 16 * lev, 16 * count), :] for t in range(2)], axis=1)

    def open_faces(lev, count, value):
        rows = []
        for k in range(count):
            rows.append(jnp.concatenate(
                [jnp.where(dm_x[t] > float(lev + k), value[16 * k:16 * k + 16, 128 * t:128 * t + 128], 0.0)
                 for t in range(2)], axis=1))
        return jnp.concatenate(rows, axis=0)

    def explicit_levels(src, lev0, count, dst):
        td = matmul(wide(src, lev0, count), 0, 2)
        gx = open_faces(lev0, count, wide(xbuf, lev0, count) * td[:, :256] - 1.2 * td[:, 256:])
        ax = matmul(gx, 2, 1)
        for k in range(count):
            lev = lev0 + k
            for t in range(2):
                c = get(src, t, lev)
                ym1 = get(src, t, lev, -1)
                ym2 = jnp.where(row_lo2, 0.0, get(src, t, lev, -2))
                yp1 = jnp.where(row15, 0.0, get(src, t, lev, 1))
                gy = jnp.where(dm_y[t] > float(lev),
                               get(ybuf, t, lev) * (7.0 * (c + ym1) - (yp1 + ym2)) - 1.2 * (c - ym1), 0.0)
                gyp = roll(gy, 15, 0)
                put(dst, t, lev, c * (1.0 - 0.2 * c)
                    + (ax[16 * k:16 * k + 16, 128 * t:128 * t + 128] + (gy - gyp)) * TWELFTH)

    def adjoint_levels(src, lev0, count, dst, extra):
        j = open_faces(lev0, count, matmul(wide(src, lev0, count), 1, 1))
        ax = matmul(wide(xbuf, lev0, count) * j, 3, 1) - matmul(1.2 * j, 2, 1)
        for k in range(count):
            lev = lev0 + k
            for t in range(2):
                g = get(src, t, lev)
                jy = jnp.where(dm_y[t] > float(lev), g - get(src, t, lev, -1), 0.0)
                cy = get(ybuf, t, lev) * jy
                uy = 7.0 * cy + 1.2 * jy
                wy = 7.0 * cy - 1.2 * jy
                uyp = roll(uy, 15, 0)
                cym = jnp.where(row0, 0.0, roll(cy, 1, 0))
                cyp = jnp.where(row_hi2, 0.0, roll(cy, 14, 0))
                total = ax[16 * k:16 * k + 16, 128 * t:128 * t + 128] + ((wy + uyp) - (cym + cyp))
                put(dst, t, lev, extra(t, lev, g) + total * TWELFTH)

    def over_levels(body):
        for lev in range(0, LEV, CHUNK):
            body(lev)

    over_levels(lambda lev: explicit_levels(cbuf, lev, CHUNK, ebuf))
    over_levels(lambda lev: adjoint_levels(gbuf, lev, CHUNK, rbuf, lambda t, l, g: g))

    arrive(msg_e, COLS)
    is2 = part == 2
    low = part < 2
    sp_l = rl_e[pl.ds(8, 8), :]
    sp_r = rr_e[pl.ds(8, 8), :]
    dp_l = rl_e[pl.ds(16, 8), :]
    dp_r = rr_e[pl.ds(16, 8), :]
    d_near = jnp.where(low, roll(dp_r, -1, 1), roll(dp_l, 1, 1))
    open_pk = jnp.minimum(dp, d_near) > levlane
    af_pk = jnp.where(open_pk, jnp.where(low, roll(sp_r, -1, 1), s_pk), 0.0)
    bf_pk = jnp.where(open_pk, 1.2, 0.0)
    a_next = roll(a_pk, -1, 1)

    def explicit_rows(ref, base, rows, ru, rd):
        for t in range(2):
            c2 = ru[pl.ds(16 * t, 16), :]
            c1 = ru[pl.ds(32 + 16 * t, 16), :]
            n0 = rd[pl.ds(16 * t, 16), :]
            n1 = rd[pl.ds(32 + 16 * t, 16), :]
            r0, r1, r14, r15 = (rows[r][t] for r in (0, 1, 14, 15))
            g0 = a0[t] * (7.0 * (r0 + c1) - (r1 + c2)) - b0[t] * (r0 - c1)
            gn = an[t] * (7.0 * (n0 + r15) - (n1 + r14)) - bn[t] * (n0 - r15)
            p = a1[t] * c1
            q = a15[t] * n0
            row_put(ref, t, 0, base[0][t] + (g0 + p) * TWELFTH)
            row_put(ref, t, 1, base[1][t] + p * -TWELFTH)
            row_put(ref, t, 14, base[14][t] + q * TWELFTH)
            row_put(ref, t, 15, base[15][t] + (q + gn) * -TWELFTH)

    def explicit_cols(c, rl, rr):
        cl = rl[pl.ds(0, 8), :]
        cr = rr[pl.ds(0, 8), :]
        x1, x2 = roll(cl, 1, 1), roll(cl, 2, 1)
        y1, y2 = roll(cr, -1, 1), roll(cr, -2, 1)
        near = jnp.where(low, y1, x1)
        far = jnp.where(low, y2 + roll(c, 1, 1), x2 + roll(c, -1, 1))
        step = jnp.where(low, y1 - c, c - x1)
        face = af_pk * (7.0 * (c + near) - far) - bf_pk * step
        return TWELFTH * jnp.where(
            part == 0, a_next * y2,
            jnp.where(part == 1, -(a_pk * y1 + face),
                      jnp.where(part == 2, face + a_next * x1, -(a_pk * x2))))

    def adjoint_rows(ref, base, rows, ru, rd):
        for t in range(2):
            gu = ru[pl.ds(16 * t, 16), :]
            cu = ru[pl.ds(32 + 16 * t, 16), :]
            gd = rd[pl.ds(16 * t, 16), :]
            cd = rd[pl.ds(32 + 16 * t, 16), :]
            j0 = rows[0][t] - gu
            jn = gd - rows[15][t]
            f0 = a0[t] * j0
            fn = an[t] * jn
            row_put(ref, t, 0, base[0][t] + (7.0 * f0 - cu - b0[t] * j0) * TWELFTH)
            row_put(ref, t, 1, base[1][t] + f0 * -TWELFTH)
            row_put(ref, t, 14, base[14][t] + fn * -TWELFTH)
            row_put(ref, t, 15, base[15][t] + (7.0 * fn - cd + bn[t] * jn) * TWELFTH)

    def adjoint_cols(g, rl, rr):
        gl = rl[pl.ds(0, 8), :]
        kl = rl[pl.ds(8, 8), :]
        gr = rr[pl.ds(0, 8), :]
        kr = rr[pl.ds(8, 8), :]
        j = jnp.where(low, roll(gr, -1, 1) - g, g - roll(gl, 1, 1))
        f = af_pk * j
        s = bf_pk * j
        outer = jnp.where(low, roll(kr, -2, 1), roll(kl, 1, 1))
        edge = 7.0 * f - outer + jnp.where(low, s, -s)
        inner = -jnp.where(low, roll(f, -1, 1), roll(f, 1, 1))
        return TWELFTH * jnp.where((part == 1) | is2, edge, inner)

    lane_lo2_8 = lane8 < 2
    lane_hi2_8 = lane8 >= 126

    def add_cols(ref, packed, extra):
        for lev in range(LEV):
            both = with_cols(ref, packed, lev)
            for t in range(2):
                put(ref, t, lev, extra(t, lev, both[t]))

    def with_cols(ref, packed, lev):
        halves = [roll(packed, 126 - 4 * (2 * lev + k), 1) for k in range(2)]
        left = jnp.concatenate([jnp.where(lane_lo2_8, h, 0.0) for h in halves], axis=0)
        right = jnp.concatenate([jnp.where(lane_hi2_8, h, 0.0) for h in halves], axis=0)
        return [get(ref, 0, lev) + left, get(ref, 1, lev) + right]

    def plain(t, lev, value):
        return value

    def solve_explicit(out_ref):
        last = forward(lambda lev: [masked(t, lev, get(ebuf, t, lev)) for t in range(2)], qbuf)
        backward(qbuf, last, plain, out_ref)

    add_cols(ebuf, explicit_cols(c_pk, rl_e, rr_e), plain)
    base = edge_rows(ebuf)
    arrive(msg_e, LINES)
    du = [jnp.broadcast_to(ru_e[pl.ds(64 + t, 1), :], (16, 128)) for t in range(2)]
    dd = [jnp.broadcast_to(rd_e[pl.ds(96 + t, 1), :], (16, 128)) for t in range(2)]
    open0 = [jnp.minimum(du[t], d_rows[0][t]) > levrow for t in range(2)]
    openn = [jnp.minimum(dd[t], d_rows[15][t]) > levrow for t in range(2)]
    a0 = [jnp.where(open0[t], s_rows[0][t], 0.0) for t in range(2)]
    an = [jnp.where(openn[t], rd_e[pl.ds(64 + 16 * t, 16), :], 0.0) for t in range(2)]
    b0 = [jnp.where(open0[t], 1.2, 0.0) for t in range(2)]
    bn = [jnp.where(openn[t], 1.2, 0.0) for t in range(2)]
    explicit_rows(ebuf, base, c_rows, ru_e, rd_e)
    solve_explicit(sbuf)

    f_rows = edge_rows(sbuf)
    for t in range(2):
        dn_a[pl.ds(16 * t, 16), :] = f_rows[14][t]
        dn_a[pl.ds(32 + 16 * t, 16), :] = f_rows[15][t]
        up_a[pl.ds(16 * t, 16), :] = f_rows[0][t]
        up_a[pl.ds(32 + 16 * t, 16), :] = f_rows[1][t]
    start(msg_a, LINES)
    f_pk = pack(sbuf)
    px_a[...] = f_pk
    start(msg_a, COLS)

    arrive(msg_l, COLS)
    l_cols = adjoint_cols(g_pk, rl_l, rr_l)
    base = edge_rows(rbuf)
    arrive(msg_l, LINES)
    adjoint_rows(rbuf, base, g_rows, ru_l, rd_l)

    def read_adjoint(lev):
        both = with_cols(rbuf, l_cols, lev)
        return [both[t] - 0.4 * get(sbuf, t, lev) * get(gbuf, t, lev) for t in range(2)]

    last = forward(read_adjoint, qbuf)
    backward(qbuf, last, masked, g2buf)
    h_rows = send_rows(g2buf, dn_b, up_b, msg_b)
    h_pk = send_cols(g2buf, px_b, msg_b)

    over_levels(lambda lev: explicit_levels(sbuf, lev, CHUNK, ebuf))
    over_levels(lambda lev: adjoint_levels(
        g2buf, lev, CHUNK, rbuf, lambda t, l, g: g * (1.0 - 0.4 * get(cbuf, t, l))))

    arrive(msg_a, COLS)
    add_cols(ebuf, explicit_cols(f_pk, rl_a, rr_a), plain)
    arrive(msg_b, COLS)
    add_cols(rbuf, adjoint_cols(h_pk, rl_b, rr_b), plain)
    base = edge_rows(ebuf)
    arrive(msg_a, LINES)
    explicit_rows(ebuf, base, f_rows, ru_a, rd_a)
    solve_explicit(final)

    base = edge_rows(rbuf)
    arrive(msg_b, LINES)
    adjoint_rows(rbuf, base, h_rows, ru_b, rd_b)

    for msg in (msg_e, msg_l, msg_a, msg_b):
        for who in SIDES:
            @pl.when(has[who])
            def _():
                msg[who].wait_send()


def flush_kernel(final, adjoint, fin_hbm, adj_hbm, sem):
    copies = []
    for n, (src, dst) in enumerate(((final, fin_hbm), (adjoint, adj_hbm))):
        for t in range(2):
            copies.append(pltpu.make_async_copy(
                src.at[pl.ds(t * PR + PAD, FLAT), :], dst.at[:, pl.ds(128 * t, 128)], sem.at[n, t]))
    for copy in copies:
        copy.start()
    for copy in copies:
        copy.wait()


def solution(mesh):
    n_group, n_tile = mesh.shape["group"], mesh.shape["tile"]

    def shards(tracer, east_speed, north_speed, mixing, depth_levels, sensitivity):
        lev, rows, cols = tracer.shape

        def flat(x):
            return x.reshape(-1, cols)

        def vm(n):
            return pltpu.VMEM((n, 128), F32)

        big = 2 * PR
        hbm = pl.BlockSpec(memory_space=pltpu.HBM)
        vmem = pl.BlockSpec(memory_space=pltpu.VMEM)
        out = pl.pallas_call(
            functools.partial(kernel, n_group, n_tile),
            out_shape=[jax.ShapeDtypeStruct((big, 128), F32)] * 2,
            in_specs=[hbm] * 6,
            out_specs=[vmem] * 2,
            scratch_shapes=(
                [vm(big)] * 9 + [pltpu.VMEM((32, 128), jnp.int32)] + [vm(big)] * 3
                + [vm(72), vm(104), vm(64), vm(64), vm(64), vm(64), vm(64), vm(64)]
                + [vm(24), vm(16), vm(8), vm(16)]
                + [vm(72), vm(104), vm(64), vm(64), vm(64), vm(64), vm(64), vm(64)]
                + [vm(24), vm(24), vm(16), vm(16), vm(8), vm(8), vm(16), vm(16)]
                + [pltpu.VMEM((256, 1024), jnp.bfloat16), pltpu.SemaphoreType.DMA((6, 2)),
                   pltpu.SemaphoreType.DMA((4, 4)), pltpu.SemaphoreType.DMA((4, 4))]
            ),
            compiler_params=pltpu.CompilerParams(collective_id=0, has_side_effects=True, vmem_limit_bytes=VMEM_MAIN),
        )(*[pltpu.with_memory_space_constraint(x, pltpu.HBM) for x in (
            flat(tracer), flat(east_speed), flat(north_speed), flat(mixing), depth_levels, flat(sensitivity))])
        out = pl.pallas_call(
            flush_kernel,
            out_shape=[jax.ShapeDtypeStruct((lev * rows, cols), F32)] * 2,
            in_specs=[vmem] * 2,
            out_specs=[hbm] * 2,
            scratch_shapes=[pltpu.SemaphoreType.DMA((2, 2))],
            compiler_params=pltpu.CompilerParams(vmem_limit_bytes=VMEM_FLUSH),
        )(*out)
        return tuple(o.reshape(lev, rows, cols) for o in out)

    spec = P(None, "group", "tile")
    return jax.shard_map(
        shards, mesh=mesh, in_specs=(spec, spec, spec, spec, P("group", "tile"), spec),
        out_specs=(spec, spec), check_vma=False)
```
